256 devices in a mesh: img: 64 (over z, y, core), gy: 4 (over x).
Axes of the slice: x: 4, y: 4, z: 8, core: 2. Of those that a mesh axis runs over, the one named last changes fastest.
Arguments:
- path: float32 [256, 4, 128, 128], P('img', None, 'gy'), may hold values from -1.2 to 1.2
- start_image: float32 [4, 128, 128], P(None, 'gy'), may hold values from -1.2 to 1.2
- end_image: float32 [4, 128, 128], P(None, 'gy'), may hold values from -1.2 to 1.2
- labels: int32 [4, 128, 128], P(None, 'gy'), may hold values from 0 to 3
- mob_table: float32 [4], replicated, may hold values from 0.2 to 2
Outputs:
- new_path: float32 [256, 4, 128, 128], P('img', None, 'gy')
The draws below stay inside these ranges and needn't reach their ends.
All inputs are finite; a program needn't handle non-finite values.
Results may differ from the reference program's by a relative error of at most 0.0001.
Values sent between devices are 32-bit elements; how exact they have to be, the bound alone decides.
A program may use at most 64 MiB of HBM per device.

```python
import math
import jax
import jax.numpy as jnp
from jax import lax

X = 4
Z = 128
LEVELS = 4
ITERS = 2
IMAGES = 256
Y = 128


def set_ends(entries, key, smallest, high):
    extent = entries.shape
    place = [jax.random.randint(jax.random.fold_in(key, axis), (), 0, extent[axis]) for axis in range(len(extent))]
    entries = entries.at[tuple(place)].set(smallest)
    longest = extent.index(max(extent))
    place[longest] = (place[longest] + 1) % extent[longest]
    return entries.at[tuple(place)].set(high)


def levels(own_key, shape, split, least, high):
    level = 1.0
    for axis_at, blocks in split:
        draws = jax.random.uniform(jax.random.fold_in(jax.random.fold_in(own_key, 6), axis_at), (blocks,), jnp.float32, least / len(split), high / len(split))
        level = level * jnp.repeat(jnp.exp(draws), shape[axis_at] // blocks).reshape((-1,) + (1,) * (len(shape) - 1 - axis_at))
    return level


def setup_inputs(seed: int = 0) -> dict:
    key_of = jax.random.split(jax.random.key(seed), 6)
    return {
        "path": jnp.clip(jax.random.uniform(key_of[0], (IMAGES, X, Y, Z), jnp.float32, -1.2, 1.2) * levels(key_of[0], (IMAGES, X, Y, Z), ((0, 64), (2, 4)), -0.4, 0.0), -1.2, 1.2),
        "start_image": jnp.clip(jax.random.uniform(key_of[1], (X, Y, Z), jnp.float32, -1.2, 1.2) * levels(key_of[1], (X, Y, Z), ((1, 4),), -0.4, 0.0), -1.2, 1.2),
        "end_image": jnp.clip(jax.random.uniform(key_of[2], (X, Y, Z), jnp.float32, -1.2, 1.2) * levels(key_of[2], (X, Y, Z), ((1, 4),), -0.4, 0.0), -1.2, 1.2),
        "labels": set_ends(jax.random.randint(key_of[3], (X, Y, Z), 0, LEVELS), jax.random.fold_in(key_of[3], 1), 0, LEVELS - 1).astype(jnp.int32),
        "mob_table": jnp.clip(jnp.exp(jax.random.uniform(key_of[4], (LEVELS,), jnp.float32, math.log(0.2), math.log(2.0))), 0.2, 2.0),
    }


time_step = 0.5
stiffness = 0.25
step_length = 0.05

def mobility(labels, table):
    result = jnp.zeros(labels.shape, jnp.float32)
    for level in range(table.shape[0]):
        result = result + jnp.where(labels == level, table[level], jnp.float32(0.0))
    return result

def pad_y(field):
    widths = [(0, 0)] * (field.ndim - 2) + [(1, 1), (0, 0)]
    return jnp.pad(field, widths)

def laplace(padded):
    centre = padded[..., 1:-1, :]
    total = jnp.roll(centre, 1, -3) + jnp.roll(centre, -1, -3)
    total = total + jnp.roll(centre, 1, -1) + jnp.roll(centre, -1, -1)
    return total + padded[..., 2:, :] + padded[..., :-2, :] - 6.0 * centre

def drift(padded, mob):
    centre = padded[..., 1:-1, :]
    return mob * (stiffness * laplace(padded) + centre - centre * centre * centre)

def reference(path, start_image, end_image, labels, mob_table):
    mob = mobility(labels, mob_table)
    count = path.shape[0]
    weights = jnp.arange(1, count + 1).astype(jnp.float32)[:, None, None, None]
    for step in range(ITERS):
        full = jnp.concatenate([start_image[None], path, end_image[None]], 0)
        force = drift(pad_y(full[:-1]), mob)
        resid = (full[1:] - full[:-1]) / time_step - force
        mres = mob * resid[1:]
        adjoint = stiffness * laplace(pad_y(mres)) + (1.0 - 3.0 * path * path) * mres
        grad = (resid[:-1] - resid[1:]) / time_step - adjoint
        weighted = weights * grad
        before_g = jnp.cumsum(grad, 0) - grad
        before_q = jnp.cumsum(weighted, 0) - weighted
        coeff = lax.optimization_barrier(jnp.sum(grad, 0)) - lax.optimization_barrier(jnp.sum(weighted, 0)) / (count + 1)
        update = time_step * time_step * (weights * coeff - weights * before_g + before_q)
        scale = step_length / jnp.sqrt(jnp.mean(update * update) + 1e-06)
        path = path - scale * update
    return path
```

```python
import jax
import jax.numpy as jnp
from jax import lax
from jax.experimental import pallas as pl
from jax.experimental.pallas import tpu as pltpu
from jax.sharding import PartitionSpec as P

ITERS = 2
NZ, NK, NX = 8, 8, 4
G = 4
stiffness = 0.25
step_length = 0.05
MESH = pl.DeviceIdType.MESH


def ring(n, d):
    return min(d % n, -d % n)


PLANE = sorted(
    [(dy, dc) for dy in range(4) for dc in range(2) if dy or dc], key=lambda o: (-ring(4, o[0]), -o[1])
)
ZS = sorted(range(1, NZ), key=lambda d: -ring(NZ, d))
NEAR = sorted(
    [(dy, dc, dx) for dy in range(4) for dc in range(2) for dx in range(NX) if dy or dc or dx],
    key=lambda o: (-ring(4, o[0]) - ring(4, o[2]), -o[1]),
)


def laplace(v, sub):
    total = jnp.concatenate([v[1:], v[:1]], 0) + jnp.concatenate([v[-1:], v[:-1]], 0)
    total = total + pltpu.roll(v, 1, 3) + pltpu.roll(v, 127, 3)
    up = pltpu.roll(v, 7, 2)
    total = total + jnp.where(sub == 7, jnp.concatenate([up[:, 1:], up[:, :1]], 1), up)
    down = pltpu.roll(v, 1, 2)
    total = total + jnp.where(sub == 0, jnp.concatenate([down[:, -1:], down[:, :-1]], 1), down)
    return total - 6.0 * v


def kernel(
    path, start, end, labels, table, out,
    own, lab, edge, nxt, prv, labx, state, vbuf, mobb,
    s1, r1, ef, s2, r2, sr, rr, ud, s3, r3, r3h, sa, ra,
    loc, init_s, init_r, snd, rcv,
):
    img, gy = lax.axis_index("img"), lax.axis_index("gy")
    z, k = img // NK, img % NK
    y, c = k // 2, k % 2
    n_img = NZ * NK
    right, left = (img + 1) % n_img, (img + n_img - 1) % n_img
    above, below = (gy + 1) % NX, (gy + NX - 1) % NX

    def member(dy, dc):
        return ((y + dy) % 4) * 2 + (c + dc) % 2

    local = [
        pltpu.make_async_copy(path, own.at[pl.ds(0, G)], loc.at[0]),
        pltpu.make_async_copy(start, own.at[G], loc.at[1]),
        pltpu.make_async_copy(end, own.at[G + 1], loc.at[2]),
        pltpu.make_async_copy(labels, lab, loc.at[3]),
    ]
    for copy in local:
        copy.start()

    barrier = pltpu.get_barrier_semaphore()

    def greet(i, x):
        pl.semaphore_signal(barrier, inc=1, device_id=(i, x), device_id_type=MESH)

    for d in ZS:
        greet(((z + d) % NZ) * NK + k, gy)
    for dy, dc, dx in NEAR:
        greet(z * NK + member(dy, dc), (gy + dx) % NX)

    @pl.when(k == 0)
    def _():
        for x in (gy, above, below):
            greet(left, x)

    @pl.when(k == NK - 1)
    def _():
        for x in (gy, above, below):
            greet(right, x)

    at_end = jnp.where((k == 0) | (k == NK - 1), 3, 0)
    for copy in local:
        copy.wait()
    pl.semaphore_wait(barrier, len(ZS) + len(NEAR) + at_end)

    to_right = jnp.where(img == n_img - 1, G, G - 1)
    to_left = jnp.where(img == 0, G + 1, 0)
    moves = [
        (own.at[to_right], edge.at[0], right, gy),
        (own.at[to_left], edge.at[1], left, gy),
        (own.at[to_right, :, 3], prv.at[0], right, above),
        (own.at[to_right, :, 0], nxt.at[0], right, below),
        (own.at[to_left, :, 3], prv.at[G + 1], left, above),
        (own.at[to_left, :, 0], nxt.at[G + 1], left, below),
        (lab.at[:, 3], labx.at[0], img, above),
        (lab.at[:, 0], labx.at[1], img, below),
        (own.at[pl.ds(0, G), :, 3], prv.at[pl.ds(1, G)], img, above),
        (own.at[pl.ds(0, G), :, 0], nxt.at[pl.ds(1, G)], img, below),
    ]
    halo = [
        pltpu.make_async_remote_copy(a, b, init_s.at[n], init_r.at[n], device_id=(i, x), device_id_type=MESH)
        for n, (a, b, i, x) in enumerate(moves)
    ]
    for copy in halo:
        copy.start()
    for copy in halo:
        copy.wait_recv()

    shape = (4, 5, 8, 128)
    sub = lax.broadcasted_iota(jnp.int32, shape, 2)
    low = lax.broadcasted_iota(jnp.int32, (4, 1, 8, 128), 2) < 4
    has_next = jnp.where(gy < NX - 1, jnp.float32(1.0), jnp.float32(0.0))
    has_prev = jnp.where(gy > 0, jnp.float32(1.0), jnp.float32(0.0))
    inside = jnp.where(low, has_next, has_prev)

    every = jnp.concatenate([lab[...], jnp.where(low, labx[1][:, None], labx[0][:, None])], 1)
    mob = jnp.zeros(shape, jnp.float32)
    for level in range(4):
        mob = jnp.where(every == level, table[level], mob)
    mobb[...] = jnp.concatenate([mob[:, :4], mob[:, 4:] * inside], 1)

    for i in range(G + 2):
        centre = edge[0] if i == 0 else edge[1] if i == G + 1 else own[i - 1]
        side = jnp.where(low, nxt[i][:, None], prv[i][:, None]) * inside
        state[i] = jnp.concatenate([centre, side], 1)

    def send(src, dst, it, n, i, x):
        copy = pltpu.make_async_remote_copy(
            src, dst, snd.at[it, n], rcv.at[it, n], device_id=(i, x), device_id_type=MESH
        )
        copy.start()

    def bytes_of(ref, sem):
        pltpu.make_async_copy(ref, ref, sem).wait()

    cells = n_img * G * 4 * 32 * NX * 128
    for it in range(ITERS):
        mob = mobb[...]
        before = None
        hs = []
        for i in range(G + 1):
            p = state[i]
            force = mob * (stiffness * laplace(p, sub) + p - p * p * p)
            r = (state[i + 1] - p) * 2.0 - force
            if i:
                m = mob * r
                adjoint = stiffness * laplace(m, sub) + (1.0 - 3.0 * p * p) * m
                hs.append(0.25 * ((before - r) * 2.0 - adjoint))
            before = r
        h1, h2, h3, h4 = hs
        v2 = -h1
        v3 = 2.0 * v2 - h2
        v4 = 2.0 * v3 - v2 - h3
        v5 = 2.0 * v4 - v3 - h4
        for n, v in enumerate((v2, v3, v4, v5)):
            vbuf[n] = v
        sums = (
            h1 + h2 + h3 + h4,
            h1 + 2.0 * h2 + 3.0 * h3 + 4.0 * h4,
            v2 + v3 + v4,
            2.0 * v2 + 3.0 * v3 + 4.0 * v4,
        )
        squares = (v2 * v2 + v3 * v3 + v4 * v4)[:, :4]
        squares = jnp.sum(jnp.sum(squares, 0), 0)
        for n, v in enumerate(sums):
            for share in range(NK):
                t = (share % 2) * 2
                s1[it, share, n] = v[share // 2, t : t + 2]
        for dy, dc in PLANE:
            other = member(dy, dc)
            send(s1.at[it, other], r1.at[it, k], it, 0, z * NK + other, gy)
        r1[it, k] = s1[it, k]
        bytes_of(r1.at[it, pl.ds(0, NK - 1)], rcv.at[it, 0])
        before_p = jnp.zeros((2, 8, 128), jnp.float32)
        before_q = before_p
        y0, y1, y2 = before_p, before_p, before_p
        for n in range(NK):
            p, q, w0, w1 = (r1[it, n, m] for m in range(4))
            f = -before_p
            e = before_q - (4.0 * n) * before_p
            ef[n, 0], ef[n, 1] = e, f
            y0 = y0 + 4.0 * e + 10.0 * f + w0
            y1 = y1 + (16.0 * n + 10.0) * e + (40.0 * n + 30.0) * f + (4.0 * n) * w0 + w1
            y2 = y2 + e * (4.0 * e + 20.0 * f + 2.0 * w0) + f * (30.0 * f + 2.0 * w1)
            before_q = before_q + (4.0 * n) * p + q
            before_p = before_p + p
        first = (z * (G * NK)).astype(jnp.float32)
        for n, v in enumerate((before_p, before_q + first * before_p, y0, y1)):
            s2[it, n] = v
            r2[it, z, n] = v
        row = jnp.sum(y2[0] + y2[1] + squares, 0, keepdims=True)
        sr[it] = row
        rr[it, z] = row
        for d in ZS:
            other = (z + d) % NZ
            send(s2.at[it], r2.at[it, z], it, 1, other * NK + k, gy)
            send(sr.at[it], rr.at[it, z], it, 2, other * NK + k, gy)
        bytes_of(r2.at[it, pl.ds(0, NZ - 1)], rcv.at[it, 1])
        bytes_of(rr.at[it, pl.ds(0, NZ - 1)], rcv.at[it, 2])
        slope = jnp.zeros((2, 8, 128), jnp.float32)
        for n in range(NZ):
            slope = slope + (r2[it, n, 0] - r2[it, n, 1] * (1.0 / (G * n_img + 1)))
        before_q = jnp.zeros((2, 8, 128), jnp.float32)
        norm = before_q
        for n in range(NZ):
            p, q, y0, y1 = (r2[it, n, m] for m in range(4))
            base = (32.0 * n) * slope + before_q
            ud[n, 0], ud[n, 1] = base, slope
            norm = norm + base * (32.0 * base + 1056.0 * slope + 2.0 * y0) + slope * (11440.0 * slope + 2.0 * y1)
            before_q = before_q + q
            slope = slope - p
        row = jnp.sum(norm[0] + norm[1], 0, keepdims=True)
        for n in range(NZ):
            row = row + rr[it, n]
        sa[it] = row
        for n, (dy, dc, dx) in enumerate(NEAR):
            send(sa.at[it], ra.at[it, n], it, 3, z * NK + member(dy, dc), (gy + dx) % NX)
        base, slope = ud[z, 0], ud[z, 1]
        for n in range(NK):
            s3[it, n, 0] = base + (4.0 * n) * slope + ef[n, 0]
            s3[it, n, 1] = slope + ef[n, 1]
        if it < ITERS - 1:
            half = k % 2
            toward = jnp.where(half == 0, below, above)
            for dy, dc in [*PLANE, (0, 0)]:
                other = member(dy, dc)
                send(s3.at[it, other, :, half], r3h.at[k], it, 5, z * NK + other, toward)
        for dy, dc in PLANE:
            other = member(dy, dc)
            send(s3.at[it, other], r3.at[it, k], it, 4, z * NK + other, gy)
        r3[it, k] = s3[it, k]
        bytes_of(r3.at[it, pl.ds(0, NK - 1)], rcv.at[it, 4])
        if it < ITERS - 1:
            bytes_of(r3h, rcv.at[it, 5])
        bytes_of(ra.at[it], rcv.at[it, 3])
        total = sa[it]
        for n in range(len(NEAR)):
            total = total + ra[it, n]
        mean = jnp.maximum(jnp.sum(total, 1, keepdims=True), 0.0) * (1.0 / cells)
        scale = step_length / jnp.sqrt(mean + 1e-06)

        def gathered(n):
            return jnp.concatenate(
                [jnp.concatenate([r3[it, 2 * x, n], r3[it, 2 * x + 1, n]], 0)[None] for x in range(4)], 0
            )

        begin, slope = gathered(0), gathered(1)
        if it == ITERS - 1:
            for i in range(1, G + 1):
                u = begin + float(i) * slope
                if i > 1:
                    u = u + vbuf[i - 2, :, pl.ds(0, 4)]
                out[i - 1] = state[i, :, pl.ds(0, 4)] - scale * u
        else:
            side = [
                jnp.concatenate(
                    [jnp.where(low[0], r3h[2 * x, n][None], r3h[2 * x + 1, n][None])[None] for x in range(4)], 0
                )
                for n in range(2)
            ]
            begin = jnp.concatenate([begin, side[0]], 1)
            slope = jnp.concatenate([slope, side[1]], 1)
            ones = jnp.ones((4, 4, 8, 128), jnp.float32)
            step = scale * jnp.concatenate([ones, inside], 1)
            last = jnp.where(img == n_img - 1, jnp.float32(0.0), jnp.float32(1.0))
            for i in range(G + 2):
                u = begin + float(i) * slope
                if i > 1:
                    u = u + vbuf[i - 2]
                if i == G + 1:
                    u = u * last
                state[i] = state[i] - step * u

    for copy in halo:
        copy.wait_send()
    for it in range(ITERS):
        bytes_of(s1.at[it, pl.ds(0, NK - 1)], snd.at[it, 0])
        bytes_of(r2.at[it, pl.ds(0, NZ - 1)], snd.at[it, 1])
        bytes_of(rr.at[it, pl.ds(0, NZ - 1)], snd.at[it, 2])
        bytes_of(ra.at[it], snd.at[it, 3])
        bytes_of(s3.at[it, pl.ds(0, NK - 1)], snd.at[it, 4])
        if it < ITERS - 1:
            bytes_of(r3h, snd.at[it, 5])


def per_device(path, start_image, end_image, labels, mob_table):
    f32 = jnp.float32
    hbm = pl.BlockSpec(memory_space=pl.ANY)
    vmem = [
        ((G + 2, 4, 4, 8, 128), f32), ((4, 4, 8, 128), jnp.int32), ((2, 4, 4, 8, 128), f32),
        ((G + 2, 4, 8, 128), f32), ((G + 2, 4, 8, 128), f32), ((2, 4, 8, 128), jnp.int32),
        ((G + 2, 4, 5, 8, 128), f32), ((G, 4, 5, 8, 128), f32), ((4, 5, 8, 128), f32),
        ((ITERS, NK, 4, 2, 8, 128), f32), ((ITERS, NK, 4, 2, 8, 128), f32), ((NK, 2, 2, 8, 128), f32),
        ((ITERS, 4, 2, 8, 128), f32), ((ITERS, NZ, 4, 2, 8, 128), f32),
        ((ITERS, 1, 128), f32), ((ITERS, NZ, 1, 128), f32), ((NZ, 2, 2, 8, 128), f32),
        ((ITERS, NK, 2, 2, 8, 128), f32), ((ITERS, NK, 2, 2, 8, 128), f32), ((NK, 2, 8, 128), f32),
        ((ITERS, 1, 128), f32), ((ITERS, len(NEAR), 1, 128), f32),
    ]
    result = pl.pallas_call(
        kernel,
        out_shape=jax.ShapeDtypeStruct((G, 4, 4, 8, 128), f32),
        in_specs=[hbm] * 4 + [pl.BlockSpec(memory_space=pltpu.SMEM)],
        out_specs=pl.BlockSpec(memory_space=pltpu.VMEM),
        scratch_shapes=[pltpu.VMEM(*a) for a in vmem]
        + [
            pltpu.SemaphoreType.DMA((4,)),
            pltpu.SemaphoreType.DMA((10,)),
            pltpu.SemaphoreType.DMA((10,)),
            pltpu.SemaphoreType.DMA((ITERS, 6)),
            pltpu.SemaphoreType.DMA((ITERS, 6)),
        ],
        compiler_params=pltpu.CompilerParams(
            collective_id=0, has_side_effects=True, vmem_limit_bytes=32 * 2**20
        ),
        name="descent",
    )(
        path.reshape(G, 4, 4, 8, 128),
        start_image.reshape(4, 4, 8, 128),
        end_image.reshape(4, 4, 8, 128),
        labels.reshape(4, 4, 8, 128),
        mob_table,
    )
    return result.reshape(path.shape)


def solution(mesh):
    field = P(None, "gy", None)
    return jax.shard_map(
        per_device,
        mesh=mesh,
        in_specs=(P("img", None, "gy", None), field, field, field, P()),
        out_specs=P("img", None, "gy", None),
        check_vma=False,
    )
```

```python
import jax
import jax.numpy as jnp
from jax import lax
from jax.experimental import pallas as pl
from jax.experimental.pallas import tpu as pltpu
from jax.sharding import PartitionSpec as P

ITERS = 2
NZ, NK, NX = 8, 8, 4
G = 4
stiffness = 0.25
step_length = 0.05
MESH = pl.DeviceIdType.MESH


def ring(n, d):
    return min(d % n, -d % n)


PLANE = sorted(
    [(dy, dc) for dy in range(4) for dc in range(2) if dy or dc], key=lambda o: (-ring(4, o[0]), -o[1])
)
ZS = sorted(range(1, NZ), key=lambda d: -ring(NZ, d))
NEAR = sorted(
    [(dy, dc, dx) for dy in range(4) for dc in range(2) for dx in range(NX) if dy or dc or dx],
    key=lambda o: (-ring(4, o[0]) - ring(4, o[2]), -o[1]),
)


def six(v, sub):
    total = jnp.concatenate([v[1:], v[:1]], 0) + jnp.concatenate([v[-1:], v[:-1]], 0)
    total = total + pltpu.roll(v, 1, 3) + pltpu.roll(v, 127, 3)
    up = pltpu.roll(v, 7, 2)
    total = total + jnp.where(sub == 7, jnp.concatenate([up[:, 1:], up[:, :1]], 1), up)
    down = pltpu.roll(v, 1, 2)
    return total + jnp.where(sub == 0, jnp.concatenate([down[:, -1:], down[:, :-1]], 1), down)


def kernel(
    path, start, end, labels, levels, out,
    own, lab, edge, nxt, prv, labx, state, ubuf, mobb, made,
    s1, r1, ef, s2, r2, sr, rr, ud, s3, r3, r3h, sa, ra,
    table, loc, init_s, init_r, snd, rcv,
):
    img, gy = lax.axis_index("img"), lax.axis_index("gy")
    z, k = img // NK, img % NK
    y, c = k // 2, k % 2
    n_img = NZ * NK
    right, left = (img + 1) % n_img, (img + n_img - 1) % n_img
    above, below = (gy + 1) % NX, (gy + NX - 1) % NX

    def member(dy, dc):
        return ((y + dy) % 4) * 2 + (c + dc) % 2

    local = [
        pltpu.make_async_copy(path, own.at[pl.ds(0, G)], loc.at[0]),
        pltpu.make_async_copy(start, own.at[G], loc.at[1]),
        pltpu.make_async_copy(end, own.at[G + 1], loc.at[2]),
        pltpu.make_async_copy(labels, lab, loc.at[3]),
        pltpu.make_async_copy(levels, table, loc.at[4]),
    ]
    for copy in local:
        copy.start()

    barrier = pltpu.get_barrier_semaphore()

    def greet(i, x):
        pl.semaphore_signal(barrier, inc=1, device_id=(i, x), device_id_type=MESH)

    for d in ZS:
        greet(((z + d) % NZ) * NK + k, gy)
    for dy, dc, dx in NEAR:
        greet(z * NK + member(dy, dc), (gy + dx) % NX)

    @pl.when(k == 0)
    def _():
        for x in (gy, above, below):
            greet(left, x)

    @pl.when(k == NK - 1)
    def _():
        for x in (gy, above, below):
            greet(right, x)

    at_end = jnp.where((k == 0) | (k == NK - 1), 3, 0)
    for copy in local:
        copy.wait()
    pl.semaphore_wait(barrier, len(ZS) + len(NEAR) + at_end)

    to_right = jnp.where(img == n_img - 1, G, G - 1)
    to_left = jnp.where(img == 0, G + 1, 0)
    moves = [
        (own.at[to_right], edge.at[0], right, gy),
        (own.at[to_left], edge.at[1], left, gy),
        (own.at[to_right, :, 3], prv.at[0], right, above),
        (own.at[to_right, :, 0], nxt.at[0], right, below),
        (own.at[to_left, :, 3], prv.at[G + 1], left, above),
        (own.at[to_left, :, 0], nxt.at[G + 1], left, below),
        (lab.at[:, 3], labx.at[0], img, above),
        (lab.at[:, 0], labx.at[1], img, below),
        (own.at[pl.ds(0, G), :, 3], prv.at[pl.ds(1, G)], img, above),
        (own.at[pl.ds(0, G), :, 0], nxt.at[pl.ds(1, G)], img, below),
    ]
    halo = [
        pltpu.make_async_remote_copy(a, b, init_s.at[n], init_r.at[n], device_id=(i, x), device_id_type=MESH)
        for n, (a, b, i, x) in enumerate(moves)
    ]
    for copy in halo:
        copy.start()

    shape = (4, 5, 8, 128)
    sub = lax.broadcasted_iota(jnp.int32, shape, 2)
    low = lax.broadcasted_iota(jnp.int32, (4, 1, 8, 128), 2) < 4
    has_next = jnp.where(gy < NX - 1, jnp.float32(1.0), jnp.float32(0.0))
    has_prev = jnp.where(gy > 0, jnp.float32(1.0), jnp.float32(0.0))
    inside = jnp.where(low, has_next, has_prev)

    def arrived(names):
        for n in names:
            halo[n].wait_recv()

    def fill(i):
        centre = edge[0] if i == 0 else edge[1] if i == G + 1 else own[i - 1]
        side = jnp.where(low, nxt[i][:, None], prv[i][:, None]) * inside
        state[i] = jnp.concatenate([centre, side], 1)

    def send(src, dst, it, n, i, x):
        copy = pltpu.make_async_remote_copy(
            src, dst, snd.at[it, n], rcv.at[it, n], device_id=(i, x), device_id_type=MESH
        )
        copy.start()

    def bytes_of(ref, sem):
        pltpu.make_async_copy(ref, ref, sem).wait()

    def force(i):
        p = state[i]
        return mobb[...] * (stiffness * six(p, sub) - p * (0.5 + p * p))

    def residual(i, f):
        return (state[i + 1] - state[i]) * 2.0 - f

    def quarter(i, before, r):
        p = state[i]
        m = mobb[...] * r
        return 0.5 * (before - r) + ((0.125 + 0.75 * p * p) * m - 0.0625 * six(m, sub))

    cells = n_img * G * 4 * 32 * NX * 128
    zero = jnp.zeros((2, 8, 128), jnp.float32)
    for it in range(ITERS):
        if it == 0:
            arrived((6, 7))
            every = jnp.concatenate([lab[...], jnp.where(low, labx[1][:, None], labx[0][:, None])], 1)
            mob = jnp.zeros(shape, jnp.float32)
            for level in range(4):
                mob = jnp.where(every == level, table[level], mob)
            mobb[...] = jnp.concatenate([mob[:, :4], mob[:, 4:] * inside], 1)
            arrived((8, 9))
            for i in range(1, G + 1):
                fill(i)
        ra1 = residual(1, force(1))
        ra2 = residual(2, force(2))
        ra3 = residual(3, force(3))
        h2 = quarter(2, ra1, ra2)
        h3 = quarter(3, ra2, ra3)
        f4 = force(4)
        if it == 0:
            made[0], made[1], made[2], made[3], made[4] = ra1, ra3, h2, h3, f4
            arrived((1, 4, 5))
            fill(G + 1)
            arrived((0, 2, 3))
            fill(0)
            ra1, ra3, h2, h3, f4 = (made[n] for n in range(5))
        h4 = quarter(4, ra3, residual(4, f4))
        h1 = quarter(1, residual(0, force(0)), ra1)
        for n, v in enumerate((h1 + h2 + h3 + h4, h1 + 2.0 * h2 + 3.0 * h3 + 4.0 * h4)):
            for share in range(NK):
                t = (share % 2) * 2
                s1[it, share, n] = v[share // 2, t : t + 2]
        for dy, dc in PLANE:
            other = member(dy, dc)
            send(s1.at[it, other, pl.ds(0, 2)], r1.at[it, k, pl.ds(0, 2)], it, 0, z * NK + other, gy)
        v2 = -h1
        v3 = 2.0 * v2 - h2
        v4 = 2.0 * v3 - v2 - h3
        for n, v in enumerate((v2 + v3 + v4, 2.0 * v2 + 3.0 * v3 + 4.0 * v4)):
            for share in range(NK):
                t = (share % 2) * 2
                s1[it, share, 2 + n] = v[share // 2, t : t + 2]
        for dy, dc in PLANE:
            other = member(dy, dc)
            send(s1.at[it, other, pl.ds(2, 2)], r1.at[it, k, pl.ds(2, 2)], it, 1, z * NK + other, gy)
        r1[it, k] = s1[it, k]
        ubuf[2], ubuf[3], ubuf[4] = v2, v3, v4
        ubuf[5] = 2.0 * v4 - v3 - h4
        squares = (v2 * v2 + v3 * v3 + v4 * v4)[:, :4]
        squares = jnp.sum(jnp.sum(squares, 0), 0)

        bytes_of(r1.at[it, pl.ds(0, NK - 1), pl.ds(0, 2)], rcv.at[it, 0])
        sum_p, sum_q = zero, zero
        for n in range(NK):
            p, q = r1[it, n, 0], r1[it, n, 1]
            ef[n, 0], ef[n, 1] = sum_q - (4.0 * n) * sum_p, -sum_p
            sum_q = sum_q + (4.0 * n) * p + q
            sum_p = sum_p + p
        first = (z * (G * NK)).astype(jnp.float32)
        for n, v in enumerate((sum_p, sum_q + first * sum_p)):
            s2[it, n] = v
            r2[it, z, n] = v
        for d in ZS:
            other = (z + d) % NZ
            send(s2.at[it, pl.ds(0, 2)], r2.at[it, z, pl.ds(0, 2)], it, 2, other * NK + k, gy)

        bytes_of(r1.at[it, pl.ds(0, NK - 1), pl.ds(2, 2)], rcv.at[it, 1])
        y0, y1, y2 = zero, zero, zero
        for n in range(NK):
            e, f, w0, w1 = ef[n, 0], ef[n, 1], r1[it, n, 2], r1[it, n, 3]
            y0 = y0 + 4.0 * e + 10.0 * f + w0
            y1 = y1 + (16.0 * n + 10.0) * e + (40.0 * n + 30.0) * f + (4.0 * n) * w0 + w1
            y2 = y2 + e * (4.0 * e + 20.0 * f + 2.0 * w0) + f * (30.0 * f + 2.0 * w1)
        for n, v in enumerate((y0, y1)):
            s2[it, 2 + n] = v
            r2[it, z, 2 + n] = v
        row = jnp.sum(y2[0] + y2[1] + squares, 0, keepdims=True)
        sr[it] = row
        rr[it, z] = row
        for d in ZS:
            other = (z + d) % NZ
            send(s2.at[it, pl.ds(2, 2)], r2.at[it, z, pl.ds(2, 2)], it, 3, other * NK + k, gy)
            send(sr.at[it], rr.at[it, z], it, 4, other * NK + k, gy)

        bytes_of(r2.at[it, pl.ds(0, NZ - 1), pl.ds(0, 2)], rcv.at[it, 2])
        slope = zero
        for n in range(NZ):
            slope = slope + (r2[it, n, 0] - r2[it, n, 1] * (1.0 / (G * n_img + 1)))
        sum_q = zero
        for n in range(NZ):
            ud[n, 0], ud[n, 1] = (32.0 * n) * slope + sum_q, slope
            sum_q = sum_q + r2[it, n, 1]
            slope = slope - r2[it, n, 0]
        base, slope = ud[z, 0], ud[z, 1]
        for n in range(NK):
            s3[it, n, 0] = base + (4.0 * n) * slope + ef[n, 0]
            s3[it, n, 1] = slope + ef[n, 1]
        if it < ITERS - 1:
            half = k % 2
            toward = jnp.where(half == 0, below, above)
            for dy, dc in [*PLANE, (0, 0)]:
                other = member(dy, dc)
                send(s3.at[it, other, :, half], r3h.at[k], it, 7, z * NK + other, toward)
        for dy, dc in PLANE:
            other = member(dy, dc)
            send(s3.at[it, other], r3.at[it, k], it, 6, z * NK + other, gy)
        r3[it, k] = s3[it, k]

        bytes_of(r2.at[it, pl.ds(0, NZ - 1), pl.ds(2, 2)], rcv.at[it, 3])
        norm = zero
        for n in range(NZ):
            base, slope = ud[n, 0], ud[n, 1]
            norm = norm + base * (32.0 * base + 1056.0 * slope + 2.0 * r2[it, n, 2])
            norm = norm + slope * (11440.0 * slope + 2.0 * r2[it, n, 3])
        row = jnp.sum(norm[0] + norm[1], 0, keepdims=True)
        bytes_of(rr.at[it, pl.ds(0, NZ - 1)], rcv.at[it, 4])
        for n in range(NZ):
            row = row + rr[it, n]
        sa[it] = row
        for n, (dy, dc, dx) in enumerate(NEAR):
            send(sa.at[it], ra.at[it, n], it, 5, z * NK + member(dy, dc), (gy + dx) % NX)

        bytes_of(r3.at[it, pl.ds(0, NK - 1)], rcv.at[it, 6])

        def gathered(n):
            return jnp.concatenate(
                [jnp.concatenate([r3[it, 2 * x, n], r3[it, 2 * x + 1, n]], 0)[None] for x in range(4)], 0
            )

        begin, slope = gathered(0), gathered(1)
        if it == ITERS - 1:
            for i in range(1, G + 1):
                u = begin + float(i) * slope
                if i > 1:
                    u = u + ubuf[i, :, pl.ds(0, 4)]
                ubuf[i, :, pl.ds(0, 4)] = u
        else:
            bytes_of(r3h, rcv.at[it, 7])
            side = [
                jnp.concatenate(
                    [jnp.where(low[0], r3h[2 * x, n][None], r3h[2 * x + 1, n][None])[None] for x in range(4)], 0
                )
                * inside
                for n in range(2)
            ]
            begin = jnp.concatenate([begin, side[0]], 1)
            slope = jnp.concatenate([slope, side[1]], 1)
            last = jnp.where(img == n_img - 1, jnp.float32(0.0), jnp.float32(1.0))
            for i in range(G + 2):
                u = begin + float(i) * slope
                if i > 1:
                    v = ubuf[i]
                    u = u + jnp.concatenate([v[:, :4], v[:, 4:] * inside], 1)
                if i == G + 1:
                    u = u * last
                ubuf[i] = u

        bytes_of(ra.at[it], rcv.at[it, 5])
        total = sa[it]
        for n in range(len(NEAR)):
            total = total + ra[it, n]
        mean = jnp.maximum(jnp.sum(total, 1, keepdims=True), 0.0) * (1.0 / cells)
        scale = step_length / jnp.sqrt(mean + 1e-06)
        if it == ITERS - 1:
            for i in range(1, G + 1):
                out[i - 1] = state[i, :, pl.ds(0, 4)] - scale * ubuf[i, :, pl.ds(0, 4)]
        else:
            for i in range(G + 2):
                state[i] = state[i] - scale * ubuf[i]

    for copy in halo:
        copy.wait_send()
    for it in range(ITERS):
        bytes_of(s1.at[it, pl.ds(0, NK - 1), pl.ds(0, 2)], snd.at[it, 0])
        bytes_of(s1.at[it, pl.ds(0, NK - 1), pl.ds(2, 2)], snd.at[it, 1])
        bytes_of(r2.at[it, pl.ds(0, NZ - 1), pl.ds(0, 2)], snd.at[it, 2])
        bytes_of(r2.at[it, pl.ds(0, NZ - 1), pl.ds(2, 2)], snd.at[it, 3])
        bytes_of(rr.at[it, pl.ds(0, NZ - 1)], snd.at[it, 4])
        bytes_of(ra.at[it], snd.at[it, 5])
        bytes_of(s3.at[it, pl.ds(0, NK - 1)], snd.at[it, 6])
        if it < ITERS - 1:
            bytes_of(r3h, snd.at[it, 7])


def per_device(path, start_image, end_image, labels, mob_table):
    f32 = jnp.float32
    hbm = pl.BlockSpec(memory_space=pltpu.HBM)
    vmem = [
        ((G + 2, 4, 4, 8, 128), f32), ((4, 4, 8, 128), jnp.int32), ((2, 4, 4, 8, 128), f32),
        ((G + 2, 4, 8, 128), f32), ((G + 2, 4, 8, 128), f32), ((2, 4, 8, 128), jnp.int32),
        ((G + 2, 4, 5, 8, 128), f32), ((G + 2, 4, 5, 8, 128), f32), ((4, 5, 8, 128), f32),
        ((5, 4, 5, 8, 128), f32),
        ((ITERS, NK, 4, 2, 8, 128), f32), ((ITERS, NK, 4, 2, 8, 128), f32), ((NK, 2, 2, 8, 128), f32),
        ((ITERS, 4, 2, 8, 128), f32), ((ITERS, NZ, 4, 2, 8, 128), f32),
        ((ITERS, 1, 128), f32), ((ITERS, NZ, 1, 128), f32), ((NZ, 2, 2, 8, 128), f32),
        ((ITERS, NK, 2, 2, 8, 128), f32), ((ITERS, NK, 2, 2, 8, 128), f32), ((NK, 2, 8, 128), f32),
        ((ITERS, 1, 128), f32), ((ITERS, len(NEAR), 1, 128), f32),
    ]
    result = pl.pallas_call(
        kernel,
        out_shape=jax.ShapeDtypeStruct((G, 4, 4, 8, 128), f32),
        in_specs=[hbm] * 5,
        out_specs=pl.BlockSpec(memory_space=pltpu.VMEM),
        scratch_shapes=[pltpu.VMEM(*a) for a in vmem]
        + [
            pltpu.SMEM((4,), f32),
            pltpu.SemaphoreType.DMA((5,)),
            pltpu.SemaphoreType.DMA((10,)),
            pltpu.SemaphoreType.DMA((10,)),
            pltpu.SemaphoreType.DMA((ITERS, 8)),
            pltpu.SemaphoreType.DMA((ITERS, 8)),
        ],
        compiler_params=pltpu.CompilerParams(
            collective_id=0, has_side_effects=True, vmem_limit_bytes=32 * 2**20
        ),
        name="descent",
    )(
        *(
            pltpu.with_memory_space_constraint(v, pltpu.HBM)
            for v in (
                path.reshape(G, 4, 4, 8, 128),
                start_image.reshape(4, 4, 8, 128),
                end_image.reshape(4, 4, 8, 128),
                labels.reshape(4, 4, 8, 128),
                mob_table,
            )
        )
    )
    return result.reshape(path.shape)


def solution(mesh):
    field = P(None, "gy", None)
    return jax.shard_map(
        per_device,
        mesh=mesh,
        in_specs=(P("img", None, "gy", None), field, field, field, P()),
        out_specs=P("img", None, "gy", None),
        check_vma=False,
    )
```

```python
import jax
import jax.numpy as jnp
from jax import lax
from jax.experimental import pallas as pl
from jax.experimental.pallas import tpu as pltpu
from jax.sharding import PartitionSpec as P

ITERS = 2
NZ, NK, NX = 4, 16, 4
G = 4
SPAN = G * NK
stiffness = 0.25
step_length = 0.05
MESH = pl.DeviceIdType.MESH


def ring(n, d):
    return min(d % n, -d % n)


MEMBERS = [(dz, dy, dc) for dz in range(2) for dy in range(4) for dc in range(2)]
PLANE = sorted([m for m in MEMBERS if any(m)], key=lambda o: (-o[0] - ring(4, o[1]), -o[2]))
ZS = sorted(range(1, NZ), key=lambda d: -ring(NZ, d))
NEAR = sorted(
    [(*m, dx) for m in MEMBERS for dx in range(NX) if any(m) or dx],
    key=lambda o: (-o[0] - ring(4, o[1]) - ring(4, o[3]), -o[2]),
)


def six(ref, i, x, sub):
    v = ref[i, x]
    total = ref[i, (x + 1) % 4] + ref[i, (x + 3) % 4]
    total = total + pltpu.roll(v, 1, 2) + pltpu.roll(v, 127, 2)
    up = pltpu.roll(v, 7, 1)
    total = total + jnp.where(sub == 7, jnp.concatenate([up[1:], up[:1]], 0), up)
    down = pltpu.roll(v, 1, 1)
    return v, total + jnp.where(sub == 0, jnp.concatenate([down[-1:], down[:-1]], 0), down)


def kernel(
    path, start, end, labels, levels, out,
    own, lab, edge, nxt, prv, labx, state, ubuf, mobb, res, mres,
    s1, r1, ef, s2, r2, ud, s3, r3, r3h, sa, ra,
    table, loc, init_s, init_r, snd, rcv, relay,
):
    img, gy = lax.axis_index("img"), lax.axis_index("gy")
    z, k = img // NK, img % NK
    pair, y, c = k // 8, (k // 2) % 4, k % 2
    n_img = NZ * NK
    right, left = (img + 1) % n_img, (img + n_img - 1) % n_img
    above, below = (gy + 1) % NX, (gy + NX - 1) % NX

    def member(dz, dy, dc):
        return ((pair + dz) % 2) * 8 + ((y + dy) % 4) * 2 + (c + dc) % 2

    barrier = pltpu.get_barrier_semaphore()

    def signal(sem, i, x):
        pl.semaphore_signal(sem, inc=1, device_id=(i, x), device_id_type=MESH)

    def along_z(d):
        return ((z + d) % NZ) * NK + k

    for i in (left, right):
        for x in (above, below):
            signal(barrier, i, x)
    for d in (1, NZ - 1):
        signal(barrier, along_z(d), gy)

    @pl.when(k == 0)
    def _():
        signal(barrier, left, gy)

    @pl.when(k == NK - 1)
    def _():
        signal(barrier, right, gy)

    for x in (above, below):
        signal(barrier, img, x)
    for m in PLANE:
        signal(barrier, z * NK + member(*m), gy)

    local = [
        pltpu.make_async_copy(labels, lab, loc.at[0]),
        pltpu.make_async_copy(path, own, loc.at[1]),
        pltpu.make_async_copy(levels, table, loc.at[2]),
    ]
    for copy in local:
        copy.start()
    pl.semaphore_wait(barrier, len(PLANE) + 8 + jnp.where((k == 0) | (k == NK - 1), 1, 0))

    def halo_of(n, src, dst, i, x):
        return pltpu.make_async_remote_copy(
            src, dst, init_s.at[n], init_r.at[n], device_id=(i, x), device_id_type=MESH
        )

    def images(image, slot, i, n):
        return [
            halo_of(n, image, edge.at[min(slot, 1)], i, gy),
            halo_of(n + 1, image.at[:, 3], prv.at[slot], i, above),
            halo_of(n + 2, image.at[:, 0], nxt.at[slot], i, below),
        ]

    def begin_of(copies):
        for copy in copies:
            copy.start()

    halo = [*images(path.at[G - 1], 0, right, 0), *images(path.at[0], G + 1, left, 3)]
    halo += [
        halo_of(6, labels.at[:, 3], labx.at[0], img, above),
        halo_of(7, labels.at[:, 0], labx.at[1], img, below),
        halo_of(8, path.at[:, :, 3], prv.at[pl.ds(1, G)], img, above),
        halo_of(9, path.at[:, :, 0], nxt.at[pl.ds(1, G)], img, below),
    ]
    begin_of(halo[6:])

    @pl.when(img != n_img - 1)
    def _():
        begin_of(halo[:3])

    @pl.when(img == n_img - 1)
    def _():
        begin_of(images(start, 0, right, 0))

    @pl.when(img != 0)
    def _():
        begin_of(halo[3:6])

    @pl.when(img == 0)
    def _():
        begin_of(images(end, G + 1, left, 3))

    for i, x in ((along_z(1), gy), (along_z(NZ - 1), gy), (img, above), (img, below)):
        signal(relay.at[0], i, x)
    for copy in local:
        copy.wait()

    shape = (4, 5, 8, 128)
    sub = lax.broadcasted_iota(jnp.int32, (5, 8, 128), 1)
    low = lax.broadcasted_iota(jnp.int32, (4, 1, 8, 128), 2) < 4
    has_next = jnp.where(gy < NX - 1, jnp.float32(1.0), jnp.float32(0.0))
    has_prev = jnp.where(gy > 0, jnp.float32(1.0), jnp.float32(0.0))
    inside = jnp.where(low, has_next, has_prev)

    def arrived(names):
        for n in names:
            halo[n].wait_recv()

    def fill(i):
        centre = edge[0] if i == 0 else edge[1] if i == G + 1 else own[i - 1]
        side = jnp.where(low, nxt[i][:, None], prv[i][:, None]) * inside
        state[i] = jnp.concatenate([centre, side], 1)

    def send(src, dst, it, n, i, x):
        copy = pltpu.make_async_remote_copy(
            src, dst, snd.at[it, n], rcv.at[it, n], device_id=(i, x), device_id_type=MESH
        )
        copy.start()

    def bytes_of(ref, sem):
        pltpu.make_async_copy(ref, ref, sem).wait()

    def force(i, x):
        p, total = six(state, i, x, sub)
        return p, mobb[x] * (stiffness * total - p * (0.5 + p * p))

    def keep(i, x, p, f):
        r = (state[i + 1, x] - p) * 2.0 - f
        res[i, x] = r
        if i:
            mres[i, x] = mobb[x] * r

    def quarter(i, x):
        p = state[i, x]
        m, total = six(mres, i, x, sub)
        return 0.5 * (res[i - 1, x] - res[i, x]) + ((0.125 + 0.75 * p * p) * m - 0.0625 * total)

    cells = n_img * G * 4 * 32 * NX * 128
    zero = jnp.zeros((8, 128), jnp.float32)
    for it in range(ITERS):
        if it == 0:
            arrived((6, 7))
            every = jnp.concatenate([lab[...], jnp.where(low, labx[1][:, None], labx[0][:, None])], 1)
            mob = jnp.zeros(shape, jnp.float32)
            for level in range(4):
                mob = jnp.where(every == level, table[level], mob)
            mobb[...] = jnp.concatenate([mob[:, :4], mob[:, 4:] * inside], 1)
            arrived((8, 9))
            for i in range(1, G + 1):
                fill(i)
        for i in range(1, G):
            for x in range(4):
                keep(i, x, *force(i, x))
        for x in range(4):
            res[G, x] = force(G, x)[1]
        if it == 0:
            arrived((1, 2, 0))
            fill(0)
        for x in range(4):
            keep(0, x, *force(0, x))
        if it == 0:
            arrived((4, 5, 3))
            fill(G + 1)
            pl.semaphore_wait(relay.at[0], 4)
            for i, x in ((img, above), (img, below)):
                signal(relay.at[1], i, x)
        for x in range(4):
            keep(G, x, state[G, x], res[G, x])
        squares = jnp.zeros((4, 8, 128), jnp.float32)
        for turn in (2, 3, 1, 0):
            x = (k // 4 + turn) % 4
            h1, h2, h3, h4 = (quarter(i, x) for i in range(1, G + 1))
            v2 = -h1
            v3 = 2.0 * v2 - h2
            v4 = 2.0 * v3 - v2 - h3
            sums = (
                h1 + h2 + h3 + h4,
                h1 + 2.0 * h2 + 3.0 * h3 + 4.0 * h4,
                v2 + v3 + v4,
                2.0 * v2 + 3.0 * v3 + 4.0 * v4,
            )
            for n, v in enumerate(sums):
                for t in range(4):
                    s1[it, 4 * x + t, n] = v[t]
            for t in range(4):
                if turn or t:
                    other = 4 * x + (k + t) % 4
                    send(s1.at[it, other, pl.ds(0, 2)], r1.at[it, k, pl.ds(0, 2)], it, 0, z * NK + other, gy)
            ubuf[2, x], ubuf[3, x], ubuf[4, x], ubuf[5, x] = v2, v3, v4, 2.0 * v4 - v3 - h4
            squares = squares + (v2 * v2 + v3 * v3 + v4 * v4)[:4]
        for m in PLANE:
            other = member(*m)
            send(s1.at[it, other, pl.ds(2, 2)], r1.at[it, k, pl.ds(2, 2)], it, 1, z * NK + other, gy)
        r1[it, k] = s1[it, k]
        squares = jnp.sum(squares, 0)

        bytes_of(r1.at[it, pl.ds(0, NK - 1), pl.ds(0, 2)], rcv.at[it, 0])
        sum_p, sum_q = zero, zero
        for n in range(NK):
            p, q = r1[it, n, 0], r1[it, n, 1]
            ef[n, 0], ef[n, 1] = sum_q - (4.0 * n) * sum_p, -sum_p
            sum_q = sum_q + (4.0 * n) * p + q
            sum_p = sum_p + p
        first = (z * SPAN).astype(jnp.float32)
        for n, v in enumerate((sum_p, sum_q + first * sum_p)):
            s2[it, n] = v
            r2[it, z, n] = v
        if it == 0:
            pl.semaphore_wait(relay.at[1], 2)
        for d in ZS:
            other = (z + d) % NZ
            send(s2.at[it, pl.ds(0, 2)], r2.at[it, z, pl.ds(0, 2)], it, 2, other * NK + k, gy)

        bytes_of(r1.at[it, pl.ds(0, NK - 1), pl.ds(2, 2)], rcv.at[it, 1])
        y0, y1, y2 = zero, zero, zero
        for n in range(NK):
            e, f, w0, w1 = ef[n, 0], ef[n, 1], r1[it, n, 2], r1[it, n, 3]
            y0 = y0 + 4.0 * e + 10.0 * f + w0
            y1 = y1 + (16.0 * n + 10.0) * e + (40.0 * n + 30.0) * f + (4.0 * n) * w0 + w1
            y2 = y2 + e * (4.0 * e + 20.0 * f + 2.0 * w0) + f * (30.0 * f + 2.0 * w1)
        for n, v in enumerate((y0, y1, y2 + squares)):
            s2[it, 2 + n] = v
            r2[it, z, 2 + n] = v
        for d in ZS:
            other = (z + d) % NZ
            send(s2.at[it, pl.ds(2, 3)], r2.at[it, z, pl.ds(2, 3)], it, 3, other * NK + k, gy)

        bytes_of(r2.at[it, pl.ds(0, NZ - 1), pl.ds(0, 2)], rcv.at[it, 2])
        slope = zero
        for n in range(NZ):
            slope = slope + (r2[it, n, 0] - r2[it, n, 1] * (1.0 / (G * n_img + 1)))
        sum_q = zero
        for n in range(NZ):
            ud[n, 0], ud[n, 1] = float(SPAN * n) * slope + sum_q, slope
            sum_q = sum_q + r2[it, n, 1]
            slope = slope - r2[it, n, 0]
        base, slope = ud[z, 0], ud[z, 1]
        for n in range(NK):
            s3[it, n, 0] = base + (4.0 * n) * slope + ef[n, 0]
            s3[it, n, 1] = slope + ef[n, 1]
        if it < ITERS - 1:

            @pl.when((k % 4) % 3 == 0)
            def _(it=it):
                low_end = k % 4 == 0
                slot = (k // 4) * 2 + jnp.where(low_end, 0, 1)
                for m in MEMBERS:
                    other = member(*m)
                    send(s3.at[it, other], r3h.at[slot], it, 7, z * NK + other, jnp.where(low_end, below, above))

        for m in PLANE:
            other = member(*m)
            send(s3.at[it, other], r3.at[it, k], it, 6, z * NK + other, gy)
        r3[it, k] = s3[it, k]

        bytes_of(r2.at[it, pl.ds(0, NZ - 1), pl.ds(2, 3)], rcv.at[it, 3])
        norm = zero
        for n in range(NZ):
            base, slope = ud[n, 0], ud[n, 1]
            norm = norm + base * (float(SPAN) * base + float(SPAN * (SPAN + 1)) * slope + 2.0 * r2[it, n, 2])
            norm = norm + slope * (float(SPAN * (SPAN + 1) * (2 * SPAN + 1) // 6) * slope + 2.0 * r2[it, n, 3])
            norm = norm + r2[it, n, 4]
        row = jnp.sum(norm, 0, keepdims=True)
        sa[it] = row
        for n, (*m, dx) in enumerate(NEAR):
            send(sa.at[it], ra.at[it, n], it, 5, z * NK + member(*m), (gy + dx) % NX)

        bytes_of(r3.at[it, pl.ds(0, NK - 1)], rcv.at[it, 6])

        begin, slope = (r3[it, :, n].reshape(4, 4, 8, 128) for n in range(2))
        if it == ITERS - 1:
            for i in range(1, G + 1):
                u = begin + float(i) * slope
                if i > 1:
                    u = u + ubuf[i, :, pl.ds(0, 4)]
                ubuf[i, :, pl.ds(0, 4)] = u
        else:
            bytes_of(r3h, rcv.at[it, 7])
            side = [
                jnp.concatenate(
                    [jnp.where(low[0], r3h[2 * x, n][None], r3h[2 * x + 1, n][None])[None] for x in range(4)], 0
                )
                for n in range(2)
            ]
            begin = jnp.concatenate([begin, side[0]], 1)
            slope = jnp.concatenate([slope, side[1]], 1)
            last = jnp.where(img == n_img - 1, jnp.float32(0.0), jnp.float32(1.0))
            for i in range(G + 2):
                u = begin + float(i) * slope
                if i > 1:
                    u = u + ubuf[i]
                if i == G + 1:
                    u = u * last
                ubuf[i] = u

        bytes_of(ra.at[it], rcv.at[it, 5])
        total = sa[it]
        for n in range(len(NEAR)):
            total = total + ra[it, n]
        mean = jnp.maximum(jnp.sum(total, 1, keepdims=True), 0.0) * (1.0 / cells)
        scale = step_length / jnp.sqrt(mean + 1e-06)
        if it == ITERS - 1:
            for i in range(1, G + 1):
                out[i - 1] = state[i, :, pl.ds(0, 4)] - scale * ubuf[i, :, pl.ds(0, 4)]
        else:
            step = scale * inside
            for i in range(G + 2):
                state[i, :, pl.ds(0, 4)] = state[i, :, pl.ds(0, 4)] - scale * ubuf[i, :, pl.ds(0, 4)]
                state[i, :, pl.ds(4, 1)] = state[i, :, pl.ds(4, 1)] - step * ubuf[i, :, pl.ds(4, 1)]

    for copy in halo:
        copy.wait_send()
    for it in range(ITERS):
        bytes_of(s1.at[it, pl.ds(0, NK - 1), pl.ds(0, 2)], snd.at[it, 0])
        bytes_of(s1.at[it, pl.ds(0, NK - 1), pl.ds(2, 2)], snd.at[it, 1])
        bytes_of(r2.at[it, pl.ds(0, NZ - 1), pl.ds(0, 2)], snd.at[it, 2])
        bytes_of(r2.at[it, pl.ds(0, NZ - 1), pl.ds(2, 3)], snd.at[it, 3])
        bytes_of(ra.at[it], snd.at[it, 5])
        bytes_of(s3.at[it, pl.ds(0, NK - 1)], snd.at[it, 6])
        if it < ITERS - 1:

            @pl.when((k % 4) % 3 == 0)
            def _(it=it):
                bytes_of(s3.at[it], snd.at[it, 7])


def per_device(path, start_image, end_image, labels, mob_table):
    f32 = jnp.float32
    hbm = pl.BlockSpec(memory_space=pltpu.HBM)
    vmem = [
        ((G, 4, 4, 8, 128), f32), ((4, 4, 8, 128), jnp.int32), ((2, 4, 4, 8, 128), f32),
        ((G + 2, 4, 8, 128), f32), ((G + 2, 4, 8, 128), f32), ((2, 4, 8, 128), jnp.int32),
        ((G + 2, 4, 5, 8, 128), f32), ((G + 2, 4, 5, 8, 128), f32), ((4, 5, 8, 128), f32),
        ((G + 1, 4, 5, 8, 128), f32), ((G + 1, 4, 5, 8, 128), f32),
        ((ITERS, NK, 4, 8, 128), f32), ((ITERS, NK, 4, 8, 128), f32), ((NK, 2, 8, 128), f32),
        ((ITERS, 5, 8, 128), f32), ((ITERS, NZ, 5, 8, 128), f32), ((NZ, 2, 8, 128), f32),
        ((ITERS, NK, 2, 8, 128), f32), ((ITERS, NK, 2, 8, 128), f32), ((8, 2, 8, 128), f32),
        ((ITERS, 1, 128), f32), ((ITERS, len(NEAR), 1, 128), f32),
    ]
    result = pl.pallas_call(
        kernel,
        out_shape=jax.ShapeDtypeStruct((G, 4, 4, 8, 128), f32),
        in_specs=[hbm] * 5,
        out_specs=pl.BlockSpec(memory_space=pltpu.VMEM),
        scratch_shapes=[pltpu.VMEM(*a) for a in vmem]
        + [
            pltpu.SMEM((4,), f32),
            pltpu.SemaphoreType.DMA((3,)),
            pltpu.SemaphoreType.DMA((10,)),
            pltpu.SemaphoreType.DMA((10,)),
            pltpu.SemaphoreType.DMA((ITERS, 8)),
            pltpu.SemaphoreType.DMA((ITERS, 8)),
            pltpu.SemaphoreType.REGULAR((2,)),
        ],
        compiler_params=pltpu.CompilerParams(
            collective_id=0, has_side_effects=True, vmem_limit_bytes=32 * 2**20
        ),
        name="descent",
    )(
        *(
            pltpu.with_memory_space_constraint(v, pltpu.HBM)
            for v in (
                path.reshape(G, 4, 4, 8, 128),
                start_image.reshape(4, 4, 8, 128),
                end_image.reshape(4, 4, 8, 128),
                labels.reshape(4, 4, 8, 128),
                mob_table,
            )
        )
    )
    return result.reshape(path.shape)


def solution(mesh):
    field = P(None, "gy", None)
    return jax.shard_map(
        per_device,
        mesh=mesh,
        in_specs=(P("img", None, "gy", None), field, field, field, P()),
        out_specs=P("img", None, "gy", None),
        check_vma=False,
    )
```

```python
import jax
import jax.numpy as jnp
from jax import lax
from jax.experimental import pallas as pl
from jax.experimental.pallas import tpu as pltpu
from jax.sharding import PartitionSpec as P

ITERS = 2
NZ, NK, NX = 4, 16, 4
G = 4
SPAN = G * NK
stiffness = 0.25
step_length = 0.05
MESH = pl.DeviceIdType.MESH


def ring(n, d):
    return min(d % n, -d % n)


MEMBERS = [(dz, dy, dc) for dz in range(2) for dy in range(4) for dc in range(2)]
PLANE = sorted([m for m in MEMBERS if any(m)], key=lambda o: (-o[0] - ring(4, o[1]), -o[2]))
ZS = sorted(range(1, NZ), key=lambda d: -ring(NZ, d))
NEAR = sorted(
    [(*m, dx) for m in MEMBERS for dx in range(NX) if any(m) or dx],
    key=lambda o: (-o[0] - ring(4, o[1]) - ring(4, o[3]), -o[2]),
)


def six(ref, i, x, sub):
    v = ref[i, x]
    total = ref[i, (x + 1) % 4] + ref[i, (x + 3) % 4]
    total = total + pltpu.roll(v, 1, 2) + pltpu.roll(v, 127, 2)
    up = pltpu.roll(v, 7, 1)
    total = total + jnp.where(sub == 7, jnp.concatenate([up[1:], up[:1]], 0), up)
    down = pltpu.roll(v, 1, 1)
    return v, total + jnp.where(sub == 0, jnp.concatenate([down[-1:], down[:-1]], 0), down)


def kernel(
    path, start, end, labels, levels, out,
    own, lab, edge, nxt, prv, labx, state, ubuf, mobb, res, mres,
    s1, r1, ef, s2, r2, ud, s3, r3, r3h, sa, ra,
    table, loc, init_s, init_r, snd, rcv, relay,
):
    img, gy = lax.axis_index("img"), lax.axis_index("gy")
    z, k = img // NK, img % NK
    pair, y, c = k // 8, (k // 2) % 4, k % 2
    n_img = NZ * NK
    right, left = (img + 1) % n_img, (img + n_img - 1) % n_img
    above, below = (gy + 1) % NX, (gy + NX - 1) % NX

    def member(dz, dy, dc):
        return ((pair + dz) % 2) * 8 + ((y + dy) % 4) * 2 + (c + dc) % 2

    barrier = pltpu.get_barrier_semaphore()

    def signal(sem, i, x):
        pl.semaphore_signal(sem, inc=1, device_id=(i, x), device_id_type=MESH)

    def along_z(d):
        return ((z + d) % NZ) * NK + k

    for i in (left, right):
        for x in (above, below):
            signal(barrier, i, x)
    for d in (1, NZ - 1):
        signal(barrier, along_z(d), gy)

    @pl.when(k == 0)
    def _():
        signal(barrier, left, gy)

    @pl.when(k == NK - 1)
    def _():
        signal(barrier, right, gy)

    for x in (above, below):
        signal(barrier, img, x)
    for m in PLANE:
        signal(barrier, z * NK + member(*m), gy)

    local = [
        pltpu.make_async_copy(labels, lab, loc.at[0]),
        pltpu.make_async_copy(path, own, loc.at[1]),
        pltpu.make_async_copy(levels, table, loc.at[2]),
    ]
    for copy in local:
        copy.start()
    pl.semaphore_wait(barrier, len(PLANE) + 8 + jnp.where((k == 0) | (k == NK - 1), 1, 0))

    def halo_of(n, src, dst, i, x):
        return pltpu.make_async_remote_copy(
            src, dst, init_s.at[n], init_r.at[n], device_id=(i, x), device_id_type=MESH
        )

    def images(image, slot, i, n):
        return [
            halo_of(n, image, edge.at[min(slot, 1)], i, gy),
            halo_of(n + 1, image.at[:, 3], prv.at[slot], i, above),
            halo_of(n + 2, image.at[:, 0], nxt.at[slot], i, below),
        ]

    def begin_of(copies):
        for copy in copies:
            copy.start()

    halo = [*images(path.at[G - 1], 0, right, 0), *images(path.at[0], G + 1, left, 3)]
    halo += [
        halo_of(6, labels.at[:, 3], labx.at[0], img, above),
        halo_of(7, labels.at[:, 0], labx.at[1], img, below),
        halo_of(8, path.at[:, :, 3], prv.at[pl.ds(1, G)], img, above),
        halo_of(9, path.at[:, :, 0], nxt.at[pl.ds(1, G)], img, below),
    ]
    begin_of(halo[6:])

    @pl.when(img != n_img - 1)
    def _():
        begin_of(halo[:3])

    @pl.when(img == n_img - 1)
    def _():
        begin_of(images(start, 0, right, 0))

    @pl.when(img != 0)
    def _():
        begin_of(halo[3:6])

    @pl.when(img == 0)
    def _():
        begin_of(images(end, G + 1, left, 3))

    for i, x in ((along_z(1), gy), (along_z(NZ - 1), gy), (img, above), (img, below)):
        signal(relay.at[0], i, x)
    for copy in local:
        copy.wait()

    shape = (4, 5, 8, 128)
    sub = lax.broadcasted_iota(jnp.int32, (5, 8, 128), 1)
    low = lax.broadcasted_iota(jnp.int32, (4, 1, 8, 128), 2) < 4
    has_next = jnp.where(gy < NX - 1, jnp.float32(1.0), jnp.float32(0.0))
    has_prev = jnp.where(gy > 0, jnp.float32(1.0), jnp.float32(0.0))
    inside = jnp.where(low, has_next, has_prev)

    def arrived(names):
        for n in names:
            halo[n].wait_recv()

    def fill(i):
        centre = edge[0] if i == 0 else edge[1] if i == G + 1 else own[i - 1]
        side = jnp.where(low, nxt[i][:, None], prv[i][:, None]) * inside
        state[i] = jnp.concatenate([centre, side], 1)

    def send(src, dst, it, n, i, x):
        copy = pltpu.make_async_remote_copy(
            src, dst, snd.at[it, n], rcv.at[it, n], device_id=(i, x), device_id_type=MESH
        )
        copy.start()

    def bytes_of(ref, sem):
        pltpu.make_async_copy(ref, ref, sem).wait()

    def force(i, x):
        p, total = six(state, i, x, sub)
        return p, mobb[x] * (stiffness * total - p * (0.5 + p * p))

    def keep(i, x, p, f):
        r = (state[i + 1, x] - p) * 2.0 - f
        res[i, x] = r
        if i:
            mres[i, x] = mobb[x] * r

    def quarter(i, x, tiles):
        p = state[i, x, pl.ds(0, tiles)]
        m, total = six(mres, i, x, sub)
        moved = res[i - 1, x, pl.ds(0, tiles)] - res[i, x, pl.ds(0, tiles)]
        return 0.5 * moved + ((0.125 + 0.75 * p * p) * m[:tiles] - 0.0625 * total[:tiles])

    cells = n_img * G * 4 * 32 * NX * 128
    zero = jnp.zeros((8, 128), jnp.float32)
    for it in range(ITERS):
        if it == 0:
            arrived((6, 7))
            every = jnp.concatenate([lab[...], jnp.where(low, labx[1][:, None], labx[0][:, None])], 1)
            mob = jnp.zeros(shape, jnp.float32)
            for level in range(4):
                mob = jnp.where(every == level, table[level], mob)
            mobb[...] = jnp.concatenate([mob[:, :4], mob[:, 4:] * inside], 1)
            arrived((8, 9))
            for i in range(1, G + 1):
                fill(i)
        for i in range(1, G):
            for x in range(4):
                keep(i, x, *force(i, x))
        for x in range(4):
            res[G, x] = force(G, x)[1]
        if it == 0:
            arrived((1, 2, 0))
            fill(0)
        for x in range(4):
            keep(0, x, *force(0, x))
        if it == 0:
            arrived((4, 5, 3))
            fill(G + 1)
            pl.semaphore_wait(relay.at[0], 4)
            for i, x in ((img, above), (img, below)):
                signal(relay.at[1], i, x)
        for x in range(4):
            keep(G, x, state[G, x], res[G, x])
        squares = jnp.zeros((4, 8, 128), jnp.float32)
        for turn in (2, 3, 1, 0):
            x = (k // 4 + turn) % 4
            h1, h2, h3, h4 = (quarter(i, x, 5 if it < ITERS - 1 else 4) for i in range(1, G + 1))
            v2 = -h1
            v3 = 2.0 * v2 - h2
            v4 = 2.0 * v3 - v2 - h3
            sums = (
                h1 + h2 + h3 + h4,
                h1 + 2.0 * h2 + 3.0 * h3 + 4.0 * h4,
                v2 + v3 + v4,
                2.0 * v2 + 3.0 * v3 + 4.0 * v4,
            )
            for n, v in enumerate(sums):
                for t in range(4):
                    s1[it, 4 * x + t, n] = v[t]
            for t in range(4):
                if turn or t:
                    other = 4 * x + (k + t) % 4
                    send(s1.at[it, other, pl.ds(0, 2)], r1.at[it, k, pl.ds(0, 2)], it, 0, z * NK + other, gy)
            if it < ITERS - 1:
                ubuf[2, x], ubuf[3, x], ubuf[4, x], ubuf[5, x] = v2, v3, v4, 2.0 * v4 - v3 - h4
            else:
                for n, w in enumerate((v2, v3, v4)):
                    ubuf[2 + n, x, pl.ds(0, 4)] = w
            squares = squares + (v2 * v2 + v3 * v3 + v4 * v4)[:4]
        for m in PLANE:
            other = member(*m)
            send(s1.at[it, other, pl.ds(2, 2)], r1.at[it, k, pl.ds(2, 2)], it, 1, z * NK + other, gy)
        r1[it, k] = s1[it, k]
        squares = jnp.sum(squares, 0)

        bytes_of(r1.at[it, pl.ds(0, NK - 1), pl.ds(0, 2)], rcv.at[it, 0])
        sum_p, sum_q = zero, zero
        for n in range(NK):
            p, q = r1[it, n, 0], r1[it, n, 1]
            ef[n, 0], ef[n, 1] = sum_q - (4.0 * n) * sum_p, -sum_p
            sum_q = sum_q + (4.0 * n) * p + q
            sum_p = sum_p + p
        first = (z * SPAN).astype(jnp.float32)
        for n, v in enumerate((sum_p, sum_q + first * sum_p)):
            s2[it, n] = v
            r2[it, z, n] = v
        if it == 0:
            pl.semaphore_wait(relay.at[1], 2)
        for d in ZS:
            other = (z + d) % NZ
            send(s2.at[it, pl.ds(0, 2)], r2.at[it, z, pl.ds(0, 2)], it, 2, other * NK + k, gy)

        bytes_of(r1.at[it, pl.ds(0, NK - 1), pl.ds(2, 2)], rcv.at[it, 1])
        y0, y1, y2 = zero, zero, zero
        for n in range(NK):
            e, f, w0, w1 = ef[n, 0], ef[n, 1], r1[it, n, 2], r1[it, n, 3]
            y0 = y0 + 4.0 * e + 10.0 * f + w0
            y1 = y1 + (16.0 * n + 10.0) * e + (40.0 * n + 30.0) * f + (4.0 * n) * w0 + w1
            y2 = y2 + e * (4.0 * e + 20.0 * f + 2.0 * w0) + f * (30.0 * f + 2.0 * w1)
        for n, v in enumerate((y0, y1, y2 + squares)):
            s2[it, 2 + n] = v
            r2[it, z, 2 + n] = v
        for d in ZS:
            other = (z + d) % NZ
            send(s2.at[it, pl.ds(2, 3)], r2.at[it, z, pl.ds(2, 3)], it, 3, other * NK + k, gy)

        bytes_of(r2.at[it, pl.ds(0, NZ - 1), pl.ds(0, 2)], rcv.at[it, 2])
        slope = zero
        for n in range(NZ):
            slope = slope + (r2[it, n, 0] - r2[it, n, 1] * (1.0 / (G * n_img + 1)))
        sum_q = zero
        for n in range(NZ):
            ud[n, 0], ud[n, 1] = float(SPAN * n) * slope + sum_q, slope
            sum_q = sum_q + r2[it, n, 1]
            slope = slope - r2[it, n, 0]
        base, slope = ud[z, 0], ud[z, 1]
        for n in range(NK):
            s3[it, n, 0] = base + (4.0 * n) * slope + ef[n, 0]
            s3[it, n, 1] = slope + ef[n, 1]
        if it < ITERS - 1:

            @pl.when((k % 4) % 3 == 0)
            def _(it=it):
                low_end = k % 4 == 0
                slot = (k // 4) * 2 + jnp.where(low_end, 0, 1)
                for m in MEMBERS:
                    other = member(*m)
                    send(s3.at[it, other], r3h.at[slot], it, 7, z * NK + other, jnp.where(low_end, below, above))

        r3[it, k] = s3[it, k]

        bytes_of(r2.at[it, pl.ds(0, NZ - 1), pl.ds(2, 3)], rcv.at[it, 3])
        norm = zero
        for n in range(NZ):
            base, slope = ud[n, 0], ud[n, 1]
            norm = norm + base * (float(SPAN) * base + float(SPAN * (SPAN + 1)) * slope + 2.0 * r2[it, n, 2])
            norm = norm + slope * (float(SPAN * (SPAN + 1) * (2 * SPAN + 1) // 6) * slope + 2.0 * r2[it, n, 3])
            norm = norm + r2[it, n, 4]
        row = jnp.sum(norm, 0, keepdims=True)
        sa[it] = row
        for n, (*m, dx) in enumerate(NEAR):
            send(sa.at[it], ra.at[it, n], it, 5, z * NK + member(*m), (gy + dx) % NX)

        for m in PLANE:
            other = member(*m)
            send(s3.at[it, other], r3.at[it, k], it, 6, z * NK + other, gy)
        bytes_of(r3.at[it, pl.ds(0, NK - 1)], rcv.at[it, 6])

        begin, slope = (r3[it, :, n].reshape(4, 4, 8, 128) for n in range(2))
        if it == ITERS - 1:
            for i in range(1, G + 1):
                u = begin + float(i) * slope
                if i > 1:
                    u = u + ubuf[i, :, pl.ds(0, 4)]
                ubuf[i, :, pl.ds(0, 4)] = u
        else:
            bytes_of(r3h, rcv.at[it, 7])
            side = [
                jnp.concatenate(
                    [jnp.where(low[0], r3h[2 * x, n][None], r3h[2 * x + 1, n][None])[None] for x in range(4)], 0
                )
                for n in range(2)
            ]
            begin = jnp.concatenate([begin, side[0]], 1)
            slope = jnp.concatenate([slope, side[1]], 1)
            last = jnp.where(img == n_img - 1, jnp.float32(0.0), jnp.float32(1.0))
            for i in range(G + 2):
                u = begin + float(i) * slope
                if i > 1:
                    u = u + ubuf[i]
                if i == G + 1:
                    u = u * last
                ubuf[i] = u

        bytes_of(ra.at[it], rcv.at[it, 5])
        rows = [sa[it]] + [ra[it, n] for n in range(len(NEAR))]
        while len(rows) > 1:
            rows = [a + b for a, b in zip(rows[::2], rows[1::2])]
        mean = jnp.maximum(jnp.sum(rows[0], 1, keepdims=True), 0.0) * (1.0 / cells)
        scale = step_length * lax.rsqrt(mean + 1e-06)
        if it == ITERS - 1:
            for i in range(1, G + 1):
                out[i - 1] = state[i, :, pl.ds(0, 4)] - scale * ubuf[i, :, pl.ds(0, 4)]
        else:
            step = scale * inside
            for i in range(G + 2):
                state[i, :, pl.ds(0, 4)] = state[i, :, pl.ds(0, 4)] - scale * ubuf[i, :, pl.ds(0, 4)]
                state[i, :, pl.ds(4, 1)] = state[i, :, pl.ds(4, 1)] - step * ubuf[i, :, pl.ds(4, 1)]

    for copy in halo:
        copy.wait_send()
    for it in range(ITERS):
        bytes_of(s1.at[it, pl.ds(0, NK - 1), pl.ds(0, 2)], snd.at[it, 0])
        bytes_of(s1.at[it, pl.ds(0, NK - 1), pl.ds(2, 2)], snd.at[it, 1])
        bytes_of(r2.at[it, pl.ds(0, NZ - 1), pl.ds(0, 2)], snd.at[it, 2])
        bytes_of(r2.at[it, pl.ds(0, NZ - 1), pl.ds(2, 3)], snd.at[it, 3])
        bytes_of(ra.at[it], snd.at[it, 5])
        bytes_of(s3.at[it, pl.ds(0, NK - 1)], snd.at[it, 6])
        if it < ITERS - 1:

            @pl.when((k % 4) % 3 == 0)
            def _(it=it):
                bytes_of(s3.at[it], snd.at[it, 7])


def per_device(path, start_image, end_image, labels, mob_table):
    f32 = jnp.float32
    hbm = pl.BlockSpec(memory_space=pltpu.HBM)
    vmem = [
        ((G, 4, 4, 8, 128), f32), ((4, 4, 8, 128), jnp.int32), ((2, 4, 4, 8, 128), f32),
        ((G + 2, 4, 8, 128), f32), ((G + 2, 4, 8, 128), f32), ((2, 4, 8, 128), jnp.int32),
        ((G + 2, 4, 5, 8, 128), f32), ((G + 2, 4, 5, 8, 128), f32), ((4, 5, 8, 128), f32),
        ((G + 1, 4, 5, 8, 128), f32), ((G + 1, 4, 5, 8, 128), f32),
        ((ITERS, NK, 4, 8, 128), f32), ((ITERS, NK, 4, 8, 128), f32), ((NK, 2, 8, 128), f32),
        ((ITERS, 5, 8, 128), f32), ((ITERS, NZ, 5, 8, 128), f32), ((NZ, 2, 8, 128), f32),
        ((ITERS, NK, 2, 8, 128), f32), ((ITERS, NK, 2, 8, 128), f32), ((8, 2, 8, 128), f32),
        ((ITERS, 1, 128), f32), ((ITERS, len(NEAR), 1, 128), f32),
    ]
    result = pl.pallas_call(
        kernel,
        out_shape=jax.ShapeDtypeStruct((G, 4, 4, 8, 128), f32),
        in_specs=[hbm] * 5,
        out_specs=pl.BlockSpec(memory_space=pltpu.VMEM),
        scratch_shapes=[pltpu.VMEM(*a) for a in vmem]
        + [
            pltpu.SMEM((4,), f32),
            pltpu.SemaphoreType.DMA((3,)),
            pltpu.SemaphoreType.DMA((10,)),
            pltpu.SemaphoreType.DMA((10,)),
            pltpu.SemaphoreType.DMA((ITERS, 8)),
            pltpu.SemaphoreType.DMA((ITERS, 8)),
            pltpu.SemaphoreType.REGULAR((2,)),
        ],
        compiler_params=pltpu.CompilerParams(
            collective_id=0, has_side_effects=True, vmem_limit_bytes=32 * 2**20
        ),
        name="descent",
    )(
        *(
            pltpu.with_memory_space_constraint(v, pltpu.HBM)
            for v in (
                path.reshape(G, 4, 4, 8, 128),
                start_image.reshape(4, 4, 8, 128),
                end_image.reshape(4, 4, 8, 128),
                labels.reshape(4, 4, 8, 128),
                mob_table,
            )
        )
    )
    return result.reshape(path.shape)


def solution(mesh):
    field = P(None, "gy", None)
    return jax.shard_map(
        per_device,
        mesh=mesh,
        in_specs=(P("img", None, "gy", None), field, field, field, P()),
        out_specs=P("img", None, "gy", None),
        check_vma=False,
    )
```

```python
import jax
import jax.numpy as jnp
from jax import lax
from jax.experimental import pallas as pl
from jax.experimental.pallas import tpu as pltpu
from jax.sharding import PartitionSpec as P

ITERS = 2
NZ, NK, NX = 4, 16, 4
G = 4
SPAN = G * NK
stiffness = 0.25
step_length = 0.05
MESH = pl.DeviceIdType.MESH


def ring(n, d):
    return min(d % n, -d % n)


MEMBERS = [(dz, dy, dc) for dz in range(2) for dy in range(4) for dc in range(2)]
PLANE = sorted([m for m in MEMBERS if any(m)], key=lambda o: (-o[0] - ring(4, o[1]), -o[2]))
ZS = sorted(range(1, NZ), key=lambda d: -ring(NZ, d))
NEAR = sorted(
    [(*m, dx) for m in MEMBERS for dx in range(NX) if any(m) or dx],
    key=lambda o: (-o[0] - ring(4, o[1]) - ring(4, o[3]), -o[2]),
)


def six(ref, i, x, sub):
    v = ref[i, x]
    total = ref[i, (x + 1) % 4] + ref[i, (x + 3) % 4]
    total = total + pltpu.roll(v, 1, 2) + pltpu.roll(v, 127, 2)
    up = pltpu.roll(v, 7, 1)
    total = total + jnp.where(sub == 7, jnp.concatenate([up[1:], up[:1]], 0), up)
    down = pltpu.roll(v, 1, 1)
    return v, total + jnp.where(sub == 0, jnp.concatenate([down[-1:], down[:-1]], 0), down)


def kernel(
    path, start, end, labels, levels, out,
    own, lab, edge, nxt, prv, labx, state, ubuf, mobb, res, mres, sixp, sixu,
    s1, r1, ef, s2, r2, ud, s3, r3, r3h, sa, ra,
    table, loc, init_s, init_r, snd, rcv, relay,
):
    img, gy = lax.axis_index("img"), lax.axis_index("gy")
    z, k = img // NK, img % NK
    pair, y, c = k // 8, (k // 2) % 4, k % 2
    n_img = NZ * NK
    right, left = (img + 1) % n_img, (img + n_img - 1) % n_img
    above, below = (gy + 1) % NX, (gy + NX - 1) % NX

    def member(dz, dy, dc):
        return ((pair + dz) % 2) * 8 + ((y + dy) % 4) * 2 + (c + dc) % 2

    barrier = pltpu.get_barrier_semaphore()

    def signal(sem, i, x):
        pl.semaphore_signal(sem, inc=1, device_id=(i, x), device_id_type=MESH)

    def along_z(d):
        return ((z + d) % NZ) * NK + k

    for i in (left, right):
        for x in (above, below):
            signal(barrier, i, x)
    for d in (1, NZ - 1):
        signal(barrier, along_z(d), gy)

    @pl.when(k == 0)
    def _():
        signal(barrier, left, gy)

    @pl.when(k == NK - 1)
    def _():
        signal(barrier, right, gy)

    for x in (above, below):
        signal(barrier, img, x)
    for m in PLANE:
        signal(barrier, z * NK + member(*m), gy)

    local = [
        pltpu.make_async_copy(labels, lab, loc.at[0]),
        pltpu.make_async_copy(path, own, loc.at[1]),
        pltpu.make_async_copy(levels, table, loc.at[2]),
    ]
    for copy in local:
        copy.start()
    pl.semaphore_wait(barrier, len(PLANE) + 8 + jnp.where((k == 0) | (k == NK - 1), 1, 0))

    def halo_of(n, src, dst, i, x):
        return pltpu.make_async_remote_copy(
            src, dst, init_s.at[n], init_r.at[n], device_id=(i, x), device_id_type=MESH
        )

    def images(image, slot, i, n):
        return [
            halo_of(n, image, edge.at[min(slot, 1)], i, gy),
            halo_of(n + 1, image.at[:, 3], prv.at[slot], i, above),
            halo_of(n + 2, image.at[:, 0], nxt.at[slot], i, below),
        ]

    def begin_of(copies):
        for copy in copies:
            copy.start()

    halo = [*images(path.at[G - 1], 0, right, 0), *images(path.at[0], G + 1, left, 3)]
    halo += [
        halo_of(6, labels.at[:, 3], labx.at[0], img, above),
        halo_of(7, labels.at[:, 0], labx.at[1], img, below),
        halo_of(8, path.at[:, :, 3], prv.at[pl.ds(1, G)], img, above),
        halo_of(9, path.at[:, :, 0], nxt.at[pl.ds(1, G)], img, below),
    ]
    begin_of(halo[6:])

    @pl.when(img != n_img - 1)
    def _():
        begin_of(halo[:3])

    @pl.when(img == n_img - 1)
    def _():
        begin_of(images(start, 0, right, 0))

    @pl.when(img != 0)
    def _():
        begin_of(halo[3:6])

    @pl.when(img == 0)
    def _():
        begin_of(images(end, G + 1, left, 3))

    for i, x in ((along_z(1), gy), (along_z(NZ - 1), gy), (img, above), (img, below)):
        signal(relay.at[0], i, x)
    for copy in local:
        copy.wait()

    shape = (4, 5, 8, 128)
    sub = lax.broadcasted_iota(jnp.int32, (5, 8, 128), 1)
    low = lax.broadcasted_iota(jnp.int32, (4, 1, 8, 128), 2) < 4
    has_next = jnp.where(gy < NX - 1, jnp.float32(1.0), jnp.float32(0.0))
    has_prev = jnp.where(gy > 0, jnp.float32(1.0), jnp.float32(0.0))
    inside = jnp.where(low, has_next, has_prev)

    def arrived(names):
        for n in names:
            halo[n].wait_recv()

    def fill(i):
        centre = edge[0] if i == 0 else edge[1] if i == G + 1 else own[i - 1]
        side = jnp.where(low, nxt[i][:, None], prv[i][:, None]) * inside
        state[i] = jnp.concatenate([centre, side], 1)

    def send(src, dst, it, n, i, x):
        copy = pltpu.make_async_remote_copy(
            src, dst, snd.at[it, n], rcv.at[it, n], device_id=(i, x), device_id_type=MESH
        )
        copy.start()

    def bytes_of(ref, sem):
        pltpu.make_async_copy(ref, ref, sem).wait()

    def force(i, x, it, scale):
        if it == 0:
            p, total = six(state, i, x, sub)
            sixp[i, x] = total
        else:
            p, total = state[i, x], sixp[i, x] - scale * sixu[i, x]
        return p, mobb[x] * (stiffness * total - p * (0.5 + p * p))

    def keep(i, x, p, f):
        r = (state[i + 1, x] - p) * 2.0 - f
        res[i, x] = r
        if i:
            mres[i, x] = mobb[x] * r

    def quarter(i, x, tiles):
        p = state[i, x, pl.ds(0, tiles)]
        m, total = six(mres, i, x, sub)
        moved = res[i - 1, x, pl.ds(0, tiles)] - res[i, x, pl.ds(0, tiles)]
        return 0.5 * moved + ((0.125 + 0.75 * p * p) * m[:tiles] - 0.0625 * total[:tiles])

    cells = n_img * G * 4 * 32 * NX * 128
    zero = jnp.zeros((8, 128), jnp.float32)
    scale = None
    for it in range(ITERS):
        if it == 0:
            arrived((6, 7))
            every = jnp.concatenate([lab[...], jnp.where(low, labx[1][:, None], labx[0][:, None])], 1)
            mob = jnp.zeros(shape, jnp.float32)
            for level in range(4):
                mob = jnp.where(every == level, table[level], mob)
            mobb[...] = jnp.concatenate([mob[:, :4], mob[:, 4:] * inside], 1)
            arrived((8, 9))
            for i in range(1, G + 1):
                fill(i)
        for i in range(1, G):
            for x in range(4):
                keep(i, x, *force(i, x, it, scale))
        for x in range(4):
            res[G, x] = force(G, x, it, scale)[1]
        if it == 0:
            arrived((1, 2, 0))
            fill(0)
        for x in range(4):
            keep(0, x, *force(0, x, it, scale))
        if it == 0:
            arrived((4, 5, 3))
            fill(G + 1)
            pl.semaphore_wait(relay.at[0], 4)
            for i, x in ((img, above), (img, below)):
                signal(relay.at[1], i, x)
        for x in range(4):
            keep(G, x, state[G, x], res[G, x])
        squares = jnp.zeros((4, 8, 128), jnp.float32)
        for turn in (2, 3, 1, 0):
            x = (k // 4 + turn) % 4
            h1, h2, h3, h4 = (quarter(i, x, 5 if it < ITERS - 1 else 4) for i in range(1, G + 1))
            v2 = -h1
            v3 = 2.0 * v2 - h2
            v4 = 2.0 * v3 - v2 - h3
            sums = (
                h1 + h2 + h3 + h4,
                h1 + 2.0 * h2 + 3.0 * h3 + 4.0 * h4,
                v2 + v3 + v4,
                2.0 * v2 + 3.0 * v3 + 4.0 * v4,
            )
            for n, v in enumerate(sums):
                for t in range(4):
                    s1[it, 4 * x + t, n] = v[t]
            for t in range(4):
                if turn or t:
                    other = 4 * x + (k + t) % 4
                    send(s1.at[it, other, pl.ds(0, 2)], r1.at[it, k, pl.ds(0, 2)], it, 0, z * NK + other, gy)
            if it < ITERS - 1:
                ubuf[2, x], ubuf[3, x], ubuf[4, x], ubuf[5, x] = v2, v3, v4, 2.0 * v4 - v3 - h4
            else:
                for n, w in enumerate((v2, v3, v4)):
                    ubuf[2 + n, x, pl.ds(0, 4)] = w
            squares = squares + (v2 * v2 + v3 * v3 + v4 * v4)[:4]
        for m in PLANE:
            other = member(*m)
            send(s1.at[it, other, pl.ds(2, 2)], r1.at[it, k, pl.ds(2, 2)], it, 1, z * NK + other, gy)
        r1[it, k] = s1[it, k]
        squares = jnp.sum(squares, 0)

        bytes_of(r1.at[it, pl.ds(0, NK - 1), pl.ds(0, 2)], rcv.at[it, 0])
        sum_p, sum_q = zero, zero
        for n in range(NK):
            p, q = r1[it, n, 0], r1[it, n, 1]
            ef[n, 0], ef[n, 1] = sum_q - (4.0 * n) * sum_p, -sum_p
            sum_q = sum_q + (4.0 * n) * p + q
            sum_p = sum_p + p
        first = (z * SPAN).astype(jnp.float32)
        for n, v in enumerate((sum_p, sum_q + first * sum_p)):
            s2[it, n] = v
            r2[it, z, n] = v
        if it == 0:
            pl.semaphore_wait(relay.at[1], 2)
        for d in ZS:
            other = (z + d) % NZ
            send(s2.at[it, pl.ds(0, 2)], r2.at[it, z, pl.ds(0, 2)], it, 2, other * NK + k, gy)

        bytes_of(r1.at[it, pl.ds(0, NK - 1), pl.ds(2, 2)], rcv.at[it, 1])
        y0, y1, y2 = zero, zero, zero
        for n in range(NK):
            e, f, w0, w1 = ef[n, 0], ef[n, 1], r1[it, n, 2], r1[it, n, 3]
            y0 = y0 + 4.0 * e + 10.0 * f + w0
            y1 = y1 + (16.0 * n + 10.0) * e + (40.0 * n + 30.0) * f + (4.0 * n) * w0 + w1
            y2 = y2 + e * (4.0 * e + 20.0 * f + 2.0 * w0) + f * (30.0 * f + 2.0 * w1)
        for n, v in enumerate((y0, y1, y2 + squares)):
            s2[it, 2 + n] = v
            r2[it, z, 2 + n] = v
        for d in ZS:
            other = (z + d) % NZ
            send(s2.at[it, pl.ds(2, 3)], r2.at[it, z, pl.ds(2, 3)], it, 3, other * NK + k, gy)

        bytes_of(r2.at[it, pl.ds(0, NZ - 1), pl.ds(0, 2)], rcv.at[it, 2])
        slope = zero
        for n in range(NZ):
            slope = slope + (r2[it, n, 0] - r2[it, n, 1] * (1.0 / (G * n_img + 1)))
        sum_q = zero
        for n in range(NZ):
            ud[n, 0], ud[n, 1] = float(SPAN * n) * slope + sum_q, slope
            sum_q = sum_q + r2[it, n, 1]
            slope = slope - r2[it, n, 0]
        base, slope = ud[z, 0], ud[z, 1]
        for n in range(NK):
            s3[it, n, 0] = base + (4.0 * n) * slope + ef[n, 0]
            s3[it, n, 1] = slope + ef[n, 1]
        if it < ITERS - 1:

            @pl.when((k % 4) % 3 == 0)
            def _(it=it):
                low_end = k % 4 == 0
                slot = (k // 4) * 2 + jnp.where(low_end, 0, 1)
                for m in MEMBERS:
                    other = member(*m)
                    send(s3.at[it, other], r3h.at[slot], it, 7, z * NK + other, jnp.where(low_end, below, above))

        r3[it, k] = s3[it, k]

        bytes_of(r2.at[it, pl.ds(0, NZ - 1), pl.ds(2, 3)], rcv.at[it, 3])
        norm = zero
        for n in range(NZ):
            base, slope = ud[n, 0], ud[n, 1]
            norm = norm + base * (float(SPAN) * base + float(SPAN * (SPAN + 1)) * slope + 2.0 * r2[it, n, 2])
            norm = norm + slope * (float(SPAN * (SPAN + 1) * (2 * SPAN + 1) // 6) * slope + 2.0 * r2[it, n, 3])
            norm = norm + r2[it, n, 4]
        row = jnp.sum(norm, 0, keepdims=True)
        sa[it] = row
        for n, (*m, dx) in enumerate(NEAR):
            send(sa.at[it], ra.at[it, n], it, 5, z * NK + member(*m), (gy + dx) % NX)

        for m in PLANE:
            other = member(*m)
            send(s3.at[it, other], r3.at[it, k], it, 6, z * NK + other, gy)
        bytes_of(r3.at[it, pl.ds(0, NK - 1)], rcv.at[it, 6])

        begin, slope = (r3[it, :, n].reshape(4, 4, 8, 128) for n in range(2))
        if it == ITERS - 1:
            for i in range(1, G + 1):
                u = begin + float(i) * slope
                if i > 1:
                    u = u + ubuf[i, :, pl.ds(0, 4)]
                ubuf[i, :, pl.ds(0, 4)] = u
        else:
            bytes_of(r3h, rcv.at[it, 7])
            side = [
                jnp.concatenate(
                    [jnp.where(low[0], r3h[2 * x, n][None], r3h[2 * x + 1, n][None])[None] for x in range(4)], 0
                )
                for n in range(2)
            ]
            begin = jnp.concatenate([begin, side[0]], 1)
            slope = jnp.concatenate([slope, side[1]], 1)
            last = jnp.where(img == n_img - 1, jnp.float32(0.0), jnp.float32(1.0))
            for i in range(G + 2):
                u = begin + float(i) * slope
                if i > 1:
                    u = u + ubuf[i]
                if i == G + 1:
                    u = u * last
                ubuf[i] = jnp.concatenate([u[:, :4], u[:, 4:] * inside], 1)
            for i in range(G + 1):
                for x in range(4):
                    sixu[i, x] = six(ubuf, i, x, sub)[1]

        bytes_of(ra.at[it], rcv.at[it, 5])
        rows = [sa[it]] + [ra[it, n] for n in range(len(NEAR))]
        while len(rows) > 1:
            rows = [a + b for a, b in zip(rows[::2], rows[1::2])]
        mean = jnp.maximum(jnp.sum(rows[0], 1, keepdims=True), 0.0) * (1.0 / cells)
        scale = step_length * lax.rsqrt(mean + 1e-06)
        if it == ITERS - 1:
            for i in range(1, G + 1):
                out[i - 1] = state[i, :, pl.ds(0, 4)] - scale * ubuf[i, :, pl.ds(0, 4)]
        else:
            for i in range(G + 2):
                state[i] = state[i] - scale * ubuf[i]

    for copy in halo:
        copy.wait_send()
    for it in range(ITERS):
        bytes_of(s1.at[it, pl.ds(0, NK - 1), pl.ds(0, 2)], snd.at[it, 0])
        bytes_of(s1.at[it, pl.ds(0, NK - 1), pl.ds(2, 2)], snd.at[it, 1])
        bytes_of(r2.at[it, pl.ds(0, NZ - 1), pl.ds(0, 2)], snd.at[it, 2])
        bytes_of(r2.at[it, pl.ds(0, NZ - 1), pl.ds(2, 3)], snd.at[it, 3])
        bytes_of(ra.at[it], snd.at[it, 5])
        bytes_of(s3.at[it, pl.ds(0, NK - 1)], snd.at[it, 6])
        if it < ITERS - 1:

            @pl.when((k % 4) % 3 == 0)
            def _(it=it):
                bytes_of(s3.at[it], snd.at[it, 7])


def per_device(path, start_image, end_image, labels, mob_table):
    f32 = jnp.float32
    hbm = pl.BlockSpec(memory_space=pltpu.HBM)
    vmem = [
        ((G, 4, 4, 8, 128), f32), ((4, 4, 8, 128), jnp.int32), ((2, 4, 4, 8, 128), f32),
        ((G + 2, 4, 8, 128), f32), ((G + 2, 4, 8, 128), f32), ((2, 4, 8, 128), jnp.int32),
        ((G + 2, 4, 5, 8, 128), f32), ((G + 2, 4, 5, 8, 128), f32), ((4, 5, 8, 128), f32),
        *[((G + 1, 4, 5, 8, 128), f32)] * 4,
        ((ITERS, NK, 4, 8, 128), f32), ((ITERS, NK, 4, 8, 128), f32), ((NK, 2, 8, 128), f32),
        ((ITERS, 5, 8, 128), f32), ((ITERS, NZ, 5, 8, 128), f32), ((NZ, 2, 8, 128), f32),
        ((ITERS, NK, 2, 8, 128), f32), ((ITERS, NK, 2, 8, 128), f32), ((8, 2, 8, 128), f32),
        ((ITERS, 1, 128), f32), ((ITERS, len(NEAR), 1, 128), f32),
    ]
    result = pl.pallas_call(
        kernel,
        out_shape=jax.ShapeDtypeStruct((G, 4, 4, 8, 128), f32),
        in_specs=[hbm] * 5,
        out_specs=pl.BlockSpec(memory_space=pltpu.VMEM),
        scratch_shapes=[pltpu.VMEM(*a) for a in vmem]
        + [
            pltpu.SMEM((4,), f32),
            pltpu.SemaphoreType.DMA((3,)),
            pltpu.SemaphoreType.DMA((10,)),
            pltpu.SemaphoreType.DMA((10,)),
            pltpu.SemaphoreType.DMA((ITERS, 8)),
            pltpu.SemaphoreType.DMA((ITERS, 8)),
            pltpu.SemaphoreType.REGULAR((2,)),
        ],
        compiler_params=pltpu.CompilerParams(
            collective_id=0, has_side_effects=True, vmem_limit_bytes=32 * 2**20
        ),
        name="descent",
    )(
        *(
            pltpu.with_memory_space_constraint(v, pltpu.HBM)
            for v in (
                path.reshape(G, 4, 4, 8, 128),
                start_image.reshape(4, 4, 8, 128),
                end_image.reshape(4, 4, 8, 128),
                labels.reshape(4, 4, 8, 128),
                mob_table,
            )
        )
    )
    return result.reshape(path.shape)


def solution(mesh):
    field = P(None, "gy", None)
    return jax.shard_map(
        per_device,
        mesh=mesh,
        in_specs=(P("img", None, "gy", None), field, field, field, P()),
        out_specs=P("img", None, "gy", None),
        check_vma=False,
    )
```

```python
import jax
import jax.numpy as jnp
from jax import lax
from jax.experimental import pallas as pl
from jax.experimental.pallas import tpu as pltpu
from jax.sharding import PartitionSpec as P

ITERS = 2
NZ, NK, NX = 4, 16, 4
G = 4
SPAN = G * NK
stiffness = 0.25
step_length = 0.05
MESH = pl.DeviceIdType.MESH


def ring(n, d):
    return min(d % n, -d % n)


MEMBERS = [(dz, dy, dc) for dz in range(2) for dy in range(4) for dc in range(2)]
PLANE = sorted([m for m in MEMBERS if any(m)], key=lambda o: (-o[0] - ring(4, o[1]), -o[2]))
ZS = sorted(range(1, NZ), key=lambda d: -ring(NZ, d))
NEAR = sorted(
    [(*m, dx) for m in MEMBERS for dx in range(NX) if any(m) or dx],
    key=lambda o: (-o[0] - ring(4, o[1]) - ring(4, o[3]), -o[2]),
)


def six(ref, i, x, sub):
    v = ref[i, x]
    total = ref[i, (x + 1) % 4] + ref[i, (x + 3) % 4]
    total = total + pltpu.roll(v, 1, 2) + pltpu.roll(v, 127, 2)
    up = pltpu.roll(v, 7, 1)
    total = total + jnp.where(sub == 7, jnp.concatenate([up[1:], up[:1]], 0), up)
    down = pltpu.roll(v, 1, 1)
    return v, total + jnp.where(sub == 0, jnp.concatenate([down[-1:], down[:-1]], 0), down)


def kernel(
    path, start, end, labels, levels, out,
    own, lab, edge, nxt, prv, labx, state, ubuf, mobb, res, mres,
    s1, r1, ef, s2, r2, ud, s3, r3, r3h, sa, ra,
    table, loc, init_s, init_r, snd, rcv, relay,
):
    img, gy = lax.axis_index("img"), lax.axis_index("gy")
    z, k = img // NK, img % NK
    pair, y, c = k // 8, (k // 2) % 4, k % 2
    n_img = NZ * NK
    right, left = (img + 1) % n_img, (img + n_img - 1) % n_img
    above, below = (gy + 1) % NX, (gy + NX - 1) % NX

    def member(dz, dy, dc):
        return ((pair + dz) % 2) * 8 + ((y + dy) % 4) * 2 + (c + dc) % 2

    barrier = pltpu.get_barrier_semaphore()

    def signal(sem, i, x):
        pl.semaphore_signal(sem, inc=1, device_id=(i, x), device_id_type=MESH)

    def along_z(d):
        return ((z + d) % NZ) * NK + k

    for i in (left, right):
        for x in (above, below):
            signal(barrier, i, x)
    for d in (1, NZ - 1):
        signal(barrier, along_z(d), gy)

    @pl.when(k == 0)
    def _():
        signal(barrier, left, gy)

    @pl.when(k == NK - 1)
    def _():
        signal(barrier, right, gy)

    for x in (above, below):
        signal(barrier, img, x)
    for m in PLANE:
        signal(barrier, z * NK + member(*m), gy)

    local = [
        pltpu.make_async_copy(labels, lab, loc.at[0]),
        pltpu.make_async_copy(path, own, loc.at[1]),
        pltpu.make_async_copy(levels, table, loc.at[2]),
    ]
    for copy in local:
        copy.start()
    pl.semaphore_wait(barrier, len(PLANE) + 8 + jnp.where((k == 0) | (k == NK - 1), 1, 0))

    def halo_of(n, src, dst, i, x):
        return pltpu.make_async_remote_copy(
            src, dst, init_s.at[n], init_r.at[n], device_id=(i, x), device_id_type=MESH
        )

    def images(image, slot, i, n):
        return [
            halo_of(n, image, edge.at[min(slot, 1)], i, gy),
            halo_of(n + 1, image.at[:, 3], prv.at[slot], i, above),
            halo_of(n + 2, image.at[:, 0], nxt.at[slot], i, below),
        ]

    def begin_of(copies):
        for copy in copies:
            copy.start()

    halo = [*images(path.at[G - 1], 0, right, 0), *images(path.at[0], G + 1, left, 3)]
    halo += [
        halo_of(6, labels.at[:, 3], labx.at[0], img, above),
        halo_of(7, labels.at[:, 0], labx.at[1], img, below),
        halo_of(8, path.at[:, :, 3], prv.at[pl.ds(1, G)], img, above),
        halo_of(9, path.at[:, :, 0], nxt.at[pl.ds(1, G)], img, below),
    ]
    begin_of(halo[6:])

    @pl.when(img != n_img - 1)
    def _():
        begin_of(halo[:3])

    @pl.when(img == n_img - 1)
    def _():
        begin_of(images(start, 0, right, 0))

    @pl.when(img != 0)
    def _():
        begin_of(halo[3:6])

    @pl.when(img == 0)
    def _():
        begin_of(images(end, G + 1, left, 3))

    for i, x in ((along_z(1), gy), (along_z(NZ - 1), gy), (img, above), (img, below)):
        signal(relay.at[0], i, x)
    for copy in local:
        copy.wait()

    shape = (4, 5, 8, 128)
    sub = lax.broadcasted_iota(jnp.int32, (5, 8, 128), 1)
    low = lax.broadcasted_iota(jnp.int32, (4, 1, 8, 128), 2) < 4
    has_next = jnp.where(gy < NX - 1, jnp.float32(1.0), jnp.float32(0.0))
    has_prev = jnp.where(gy > 0, jnp.float32(1.0), jnp.float32(0.0))
    inside = jnp.where(low, has_next, has_prev)

    def arrived(names):
        for n in names:
            halo[n].wait_recv()

    def fill(i):
        centre = edge[0] if i == 0 else edge[1] if i == G + 1 else own[i - 1]
        side = jnp.where(low, nxt[i][:, None], prv[i][:, None]) * inside
        state[i] = jnp.concatenate([centre, side], 1)

    def send(src, dst, it, n, i, x):
        copy = pltpu.make_async_remote_copy(
            src, dst, snd.at[it, n], rcv.at[it, n], device_id=(i, x), device_id_type=MESH
        )
        copy.start()

    def bytes_of(ref, sem):
        pltpu.make_async_copy(ref, ref, sem).wait()

    def force(i, x):
        p, total = six(state, i, x, sub)
        return p, mobb[x] * (stiffness * total - p * (0.5 + p * p))

    def keep(i, x, p, f):
        r = (state[i + 1, x] - p) * 2.0 - f
        res[i, x] = r
        if i:
            mres[i, x] = mobb[x] * r

    def quarter(i, x, tiles):
        p = state[i, x, pl.ds(0, tiles)]
        m, total = six(mres, i, x, sub)
        moved = res[i - 1, x, pl.ds(0, tiles)] - res[i, x, pl.ds(0, tiles)]
        return 0.5 * moved + ((0.125 + 0.75 * p * p) * m[:tiles] - 0.0625 * total[:tiles])

    cells = n_img * G * 4 * 32 * NX * 128
    zero = jnp.zeros((8, 128), jnp.float32)
    for it in range(ITERS):
        if it == 0:
            arrived((6, 7))
            every = jnp.concatenate([lab[...], jnp.where(low, labx[1][:, None], labx[0][:, None])], 1)
            mob = jnp.zeros(shape, jnp.float32)
            for level in range(4):
                mob = jnp.where(every == level, table[level], mob)
            mobb[...] = jnp.concatenate([mob[:, :4], mob[:, 4:] * inside], 1)
            arrived((8, 9))
            for i in range(1, G + 1):
                fill(i)
        for i in range(1, G):
            for x in range(4):
                keep(i, x, *force(i, x))
        for x in range(4):
            res[G, x] = force(G, x)[1]
        if it == 0:
            arrived((1, 2, 0))
            fill(0)
        for x in range(4):
            keep(0, x, *force(0, x))
        if it == 0:
            arrived((4, 5, 3))
            fill(G + 1)
            pl.semaphore_wait(relay.at[0], 4)
            for i, x in ((img, above), (img, below)):
                signal(relay.at[1], i, x)
        for x in range(4):
            keep(G, x, state[G, x], res[G, x])
        squares = jnp.zeros((4, 8, 128), jnp.float32)
        for turn in (2, 3, 1, 0):
            x = (k // 4 + turn) % 4
            h1, h2, h3, h4 = (quarter(i, x, 5 if it < ITERS - 1 else 4) for i in range(1, G + 1))
            v2 = -h1
            v3 = 2.0 * v2 - h2
            v4 = 2.0 * v3 - v2 - h3
            sums = (
                h1 + h2 + h3 + h4,
                h1 + 2.0 * h2 + 3.0 * h3 + 4.0 * h4,
                v2 + v3 + v4,
                2.0 * v2 + 3.0 * v3 + 4.0 * v4,
            )
            for n, v in enumerate(sums):
                for t in range(4):
                    s1[it, 4 * x + t, n] = v[t]
            for t in range(4):
                if turn or t:
                    other = 4 * x + (k + t) % 4
                    send(s1.at[it, other, pl.ds(0, 2)], r1.at[it, k, pl.ds(0, 2)], it, 0, z * NK + other, gy)
            if it < ITERS - 1:
                ubuf[2, x], ubuf[3, x], ubuf[4, x], ubuf[5, x] = v2, v3, v4, 2.0 * v4 - v3 - h4
            else:
                for n, w in enumerate((v2, v3, v4)):
                    ubuf[2 + n, x, pl.ds(0, 4)] = w
            squares = squares + (v2 * v2 + v3 * v3 + v4 * v4)[:4]
        for m in PLANE:
            other = member(*m)
            send(s1.at[it, other, pl.ds(2, 2)], r1.at[it, k, pl.ds(2, 2)], it, 1, z * NK + other, gy)
        r1[it, k] = s1[it, k]
        squares = jnp.sum(squares, 0)

        bytes_of(r1.at[it, pl.ds(0, NK - 1), pl.ds(0, 2)], rcv.at[it, 0])
        sum_p, sum_q = zero, zero
        for n in range(NK):
            p, q = r1[it, n, 0], r1[it, n, 1]
            ef[n, 0], ef[n, 1] = sum_q - (4.0 * n) * sum_p, -sum_p
            sum_q = sum_q + (4.0 * n) * p + q
            sum_p = sum_p + p
        first = (z * SPAN).astype(jnp.float32)
        for n, v in enumerate((sum_p, sum_q + first * sum_p)):
            s2[it, n] = v
            r2[it, z, n] = v
        if it == 0:
            pl.semaphore_wait(relay.at[1], 2)
        for d in ZS:
            other = (z + d) % NZ
            send(s2.at[it, pl.ds(0, 2)], r2.at[it, z, pl.ds(0, 2)], it, 2, other * NK + k, gy)

        bytes_of(r1.at[it, pl.ds(0, NK - 1), pl.ds(2, 2)], rcv.at[it, 1])
        y0, y1, y2 = zero, zero, zero
        for n in range(NK):
            e, f, w0, w1 = ef[n, 0], ef[n, 1], r1[it, n, 2], r1[it, n, 3]
            y0 = y0 + 4.0 * e + 10.0 * f + w0
            y1 = y1 + (16.0 * n + 10.0) * e + (40.0 * n + 30.0) * f + (4.0 * n) * w0 + w1
            y2 = y2 + e * (4.0 * e + 20.0 * f + 2.0 * w0) + f * (30.0 * f + 2.0 * w1)
        for n, v in enumerate((y0, y1, y2 + squares)):
            s2[it, 2 + n] = v
            r2[it, z, 2 + n] = v
        for d in ZS:
            other = (z + d) % NZ
            send(s2.at[it, pl.ds(2, 3)], r2.at[it, z, pl.ds(2, 3)], it, 3, other * NK + k, gy)

        bytes_of(r2.at[it, pl.ds(0, NZ - 1), pl.ds(0, 2)], rcv.at[it, 2])
        slope = zero
        for n in range(NZ):
            slope = slope + (r2[it, n, 0] - r2[it, n, 1] * (1.0 / (G * n_img + 1)))
        sum_q = zero
        for n in range(NZ):
            ud[n, 0], ud[n, 1] = float(SPAN * n) * slope + sum_q, slope
            sum_q = sum_q + r2[it, n, 1]
            slope = slope - r2[it, n, 0]
        base, slope = ud[z, 0], ud[z, 1]
        for n in range(NK):
            s3[it, n, 0] = base + (4.0 * n) * slope + ef[n, 0]
            s3[it, n, 1] = slope + ef[n, 1]
        if it < ITERS - 1:

            @pl.when((k % 4) % 3 == 0)
            def _(it=it):
                low_end = k % 4 == 0
                slot = (k // 4) * 2 + jnp.where(low_end, 0, 1)
                for m in MEMBERS:
                    other = member(*m)
                    send(s3.at[it, other], r3h.at[slot], it, 7, z * NK + other, jnp.where(low_end, below, above))

        if it == ITERS - 1:
            for m in PLANE:
                other = member(*m)
                send(s3.at[it, other], r3.at[it, k], it, 6, z * NK + other, gy)
        r3[it, k] = s3[it, k]

        bytes_of(r2.at[it, pl.ds(0, NZ - 1), pl.ds(2, 3)], rcv.at[it, 3])
        norm = zero
        for n in range(NZ):
            base, slope = ud[n, 0], ud[n, 1]
            norm = norm + base * (float(SPAN) * base + float(SPAN * (SPAN + 1)) * slope + 2.0 * r2[it, n, 2])
            norm = norm + slope * (float(SPAN * (SPAN + 1) * (2 * SPAN + 1) // 6) * slope + 2.0 * r2[it, n, 3])
            norm = norm + r2[it, n, 4]
        row = jnp.sum(norm, 0, keepdims=True)
        sa[it] = row
        for n, (*m, dx) in enumerate(NEAR):
            send(sa.at[it], ra.at[it, n], it, 5, z * NK + member(*m), (gy + dx) % NX)

        if it < ITERS - 1:
            for m in PLANE:
                other = member(*m)
                send(s3.at[it, other], r3.at[it, k], it, 6, z * NK + other, gy)
        bytes_of(r3.at[it, pl.ds(0, NK - 1)], rcv.at[it, 6])

        begin, slope = (r3[it, :, n].reshape(4, 4, 8, 128) for n in range(2))
        if it == ITERS - 1:
            for i in range(1, G + 1):
                u = begin + float(i) * slope
                if i > 1:
                    u = u + ubuf[i, :, pl.ds(0, 4)]
                ubuf[i, :, pl.ds(0, 4)] = u
        else:
            bytes_of(r3h, rcv.at[it, 7])
            side = [
                jnp.concatenate(
                    [jnp.where(low[0], r3h[2 * x, n][None], r3h[2 * x + 1, n][None])[None] for x in range(4)], 0
                )
                for n in range(2)
            ]
            begin = jnp.concatenate([begin, side[0]], 1)
            slope = jnp.concatenate([slope, side[1]], 1)
            last = jnp.where(img == n_img - 1, jnp.float32(0.0), jnp.float32(1.0))
            for i in range(G + 2):
                u = begin + float(i) * slope
                if i > 1:
                    u = u + ubuf[i]
                if i == G + 1:
                    u = u * last
                ubuf[i] = u

        bytes_of(ra.at[it], rcv.at[it, 5])
        rows = [sa[it]] + [ra[it, n] for n in range(len(NEAR))]
        while len(rows) > 1:
            rows = [a + b for a, b in zip(rows[::2], rows[1::2])]
        mean = jnp.maximum(jnp.sum(rows[0], 1, keepdims=True), 0.0) * (1.0 / cells)
        scale = step_length * lax.rsqrt(mean + 1e-06)
        if it == ITERS - 1:
            for i in range(1, G + 1):
                out[i - 1] = state[i, :, pl.ds(0, 4)] - scale * ubuf[i, :, pl.ds(0, 4)]
        else:
            step = scale * inside
            for i in range(G + 2):
                state[i, :, pl.ds(0, 4)] = state[i, :, pl.ds(0, 4)] - scale * ubuf[i, :, pl.ds(0, 4)]
                state[i, :, pl.ds(4, 1)] = state[i, :, pl.ds(4, 1)] - step * ubuf[i, :, pl.ds(4, 1)]

    for copy in halo:
        copy.wait_send()
    for it in range(ITERS):
        bytes_of(s1.at[it, pl.ds(0, NK - 1), pl.ds(0, 2)], snd.at[it, 0])
        bytes_of(s1.at[it, pl.ds(0, NK - 1), pl.ds(2, 2)], snd.at[it, 1])
        bytes_of(r2.at[it, pl.ds(0, NZ - 1), pl.ds(0, 2)], snd.at[it, 2])
        bytes_of(r2.at[it, pl.ds(0, NZ - 1), pl.ds(2, 3)], snd.at[it, 3])
        bytes_of(ra.at[it], snd.at[it, 5])
        bytes_of(s3.at[it, pl.ds(0, NK - 1)], snd.at[it, 6])
        if it < ITERS - 1:

            @pl.when((k % 4) % 3 == 0)
            def _(it=it):
                bytes_of(s3.at[it], snd.at[it, 7])


def per_device(path, start_image, end_image, labels, mob_table):
    f32 = jnp.float32
    hbm = pl.BlockSpec(memory_space=pltpu.HBM)
    vmem = [
        ((G, 4, 4, 8, 128), f32), ((4, 4, 8, 128), jnp.int32), ((2, 4, 4, 8, 128), f32),
        ((G + 2, 4, 8, 128), f32), ((G + 2, 4, 8, 128), f32), ((2, 4, 8, 128), jnp.int32),
        ((G + 2, 4, 5, 8, 128), f32), ((G + 2, 4, 5, 8, 128), f32), ((4, 5, 8, 128), f32),
        ((G + 1, 4, 5, 8, 128), f32), ((G + 1, 4, 5, 8, 128), f32),
        ((ITERS, NK, 4, 8, 128), f32), ((ITERS, NK, 4, 8, 128), f32), ((NK, 2, 8, 128), f32),
        ((ITERS, 5, 8, 128), f32), ((ITERS, NZ, 5, 8, 128), f32), ((NZ, 2, 8, 128), f32),
        ((ITERS, NK, 2, 8, 128), f32), ((ITERS, NK, 2, 8, 128), f32), ((8, 2, 8, 128), f32),
        ((ITERS, 1, 128), f32), ((ITERS, len(NEAR), 1, 128), f32),
    ]
    result = pl.pallas_call(
        kernel,
        out_shape=jax.ShapeDtypeStruct((G, 4, 4, 8, 128), f32),
        in_specs=[hbm] * 5,
        out_specs=pl.BlockSpec(memory_space=pltpu.VMEM),
        scratch_shapes=[pltpu.VMEM(*a) for a in vmem]
        + [
            pltpu.SMEM((4,), f32),
            pltpu.SemaphoreType.DMA((3,)),
            pltpu.SemaphoreType.DMA((10,)),
            pltpu.SemaphoreType.DMA((10,)),
            pltpu.SemaphoreType.DMA((ITERS, 8)),
            pltpu.SemaphoreType.DMA((ITERS, 8)),
            pltpu.SemaphoreType.REGULAR((2,)),
        ],
        compiler_params=pltpu.CompilerParams(
            collective_id=0, has_side_effects=True, vmem_limit_bytes=32 * 2**20
        ),
        name="descent",
    )(
        *(
            pltpu.with_memory_space_constraint(v, pltpu.HBM)
            for v in (
                path.reshape(G, 4, 4, 8, 128),
                start_image.reshape(4, 4, 8, 128),
                end_image.reshape(4, 4, 8, 128),
                labels.reshape(4, 4, 8, 128),
                mob_table,
            )
        )
    )
    return result.reshape(path.shape)


def solution(mesh):
    field = P(None, "gy", None)
    return jax.shard_map(
        per_device,
        mesh=mesh,
        in_specs=(P("img", None, "gy", None), field, field, field, P()),
        out_specs=P("img", None, "gy", None),
        check_vma=False,
    )
```
